256 devices in a mesh: ia: 4 (over x), ja: 8 (over z_hi, y), ka: 8 (over z_lo, core).
Axes of the slice: x: 4, y: 4, z: 8 (z_hi: 2, z_lo: 4; z = z_hi * 4 + z_lo), core: 2. Of those that a mesh axis runs over, the one named last changes fastest.
Arguments:
- tensor: bfloat16 [1024, 1024, 1024], P('ia', 'ja', 'ka'), may hold values from -6 to 6
- factor_b: bfloat16 [1024, 256], P('ja', 'ka'), may hold values from -16 to 16
- factor_c: bfloat16 [1024, 256], P('ka', 'ja'), may hold values from -16 to 16
Outputs:
- factor_a: float32 [1024, 256], P(('ia', 'ja', 'ka'))
The draws below stay inside these ranges and needn't reach their ends.
All inputs are finite; a program needn't handle non-finite values.
Results may differ from the reference program's by a relative error of at most 0.0003.
Values may be sent and summed in bfloat16 or wider, within the bound.
A program may use at most 64 MiB of HBM per device.

```python
import jax
import jax.numpy as jnp
from jax import lax

R = 256
I = 1024
J = 1024
K = 1024


def draw_factor(key, length):
    k_place, k_shared, k_noise = jax.random.split(key, 3)
    common = 1.0
    place = (jnp.arange(length, dtype=jnp.float32) + jax.random.uniform(k_place, (length,), jnp.float32)) / length
    scales = 10.0 ** place
    shared = jnp.clip(jax.random.normal(k_shared, (length, 1), jnp.float32), -6.0, 6.0)
    noise = jnp.clip(jax.random.normal(k_noise, (length, R), jnp.float32), -6.0, 6.0)
    raw = scales[:, None] * (shared + noise)
    total = jnp.sum(scales * scales) * (common + 1.0)
    return (raw / jnp.sqrt(total)).astype(jnp.bfloat16)


def draw_factor_b(key, part):
    return draw_factor(jax.random.fold_in(key, 11), J)


def draw_factor_c(key, part):
    return draw_factor(jax.random.fold_in(key, 23), K)


def shard_levels(stream_key, extent, cuts, least, largest):
    def one(dim, blocks):
        steps = jax.random.uniform(jax.random.fold_in(jax.random.fold_in(stream_key, 6), dim), (blocks,), jnp.float32, least / len(cuts), largest / len(cuts))
        return jnp.repeat(jnp.exp(steps), extent[dim] // blocks).reshape((-1,) + (1,) * (len(extent) - dim - 1))

    level = one(*cuts[0])
    for cut in cuts[1:]:
        level = level * one(*cut)
    return level


def normal_values(own_key, dims, scale, limit, cuts=(), held_as=jnp.bfloat16):
    drawn = jax.random.normal(own_key, dims, jnp.float32) * scale
    if len(cuts) > 0:
        drawn = shard_levels(own_key, dims, cuts, -0.22, 0.18) * drawn
    return jnp.clip(drawn, min=-limit, max=limit).astype(held_as)


def setup_inputs(seed: int = 0) -> dict:
    seeds = jax.random.split(jax.random.key(seed), 4)
    return {
        "tensor": normal_values(seeds[0], (I, J, K), 1.0, 6.0, ((0, 4), (1, 8), (2, 8))),
        "factor_b": draw_factor_b(jax.random.fold_in(seeds[3], 71), 0),
        "factor_c": draw_factor_c(jax.random.fold_in(seeds[3], 71), 0),
    }


ridge_weight = 0.1

def contract(block, factor_b, factor_c):
    rows, width_j, width_k = block.shape
    inner = jnp.dot(block.reshape(rows * width_j, width_k).astype(jnp.float32), factor_c.astype(jnp.float32), preferred_element_type=jnp.float32)
    inner = inner.reshape(rows, width_j, -1)
    return jnp.sum(inner * factor_b.astype(jnp.float32)[None], axis=1)

def reference(tensor, factor_b, factor_c):
    gram_b = jnp.dot(factor_b.T.astype(jnp.float32), factor_b.astype(jnp.float32), preferred_element_type=jnp.float32)
    gram_c = jnp.dot(factor_c.T.astype(jnp.float32), factor_c.astype(jnp.float32), preferred_element_type=jnp.float32)
    normal_matrix = gram_b * gram_c + ridge_weight * jnp.eye(R, dtype=jnp.float32)
    blocks = tensor.reshape(I // 16, 16, J, K)
    mttkrp = lax.map(lambda piece: contract(piece, factor_b, factor_c), blocks).reshape(I, R)
    lower = jnp.linalg.cholesky(normal_matrix)
    solved = jax.scipy.linalg.cho_solve((lower, True), mttkrp.T)
    return solved.T
```

```python
import jax
import jax.numpy as jnp
from jax import lax
from jax.experimental import pallas as pl
from jax.experimental.pallas import tpu as pltpu
from jax.sharding import PartitionSpec as P

MESH = pl.DeviceIdType.MESH
RIDGE = 0.1
GROUP = 8
PLANE = GROUP * GROUP
RANK = 256
LANES = 128
SUB = 8
BLOCK = 16
ROWS = 256
DEPTH = 128
STEP = 8
CHUNKS = 8


def split3(x):
    a = x.astype(jnp.bfloat16)
    rest = x - a.astype(jnp.float32)
    b = rest.astype(jnp.bfloat16)
    c = (rest - b.astype(jnp.float32)).astype(jnp.bfloat16)
    return a, b, c


def eliminate(a_ref, cols_ref, w_ref, lhs_ref, rhs_ref):
    lane8 = lax.broadcasted_iota(jnp.int32, (SUB, LANES), 1)
    lane_n = lax.broadcasted_iota(jnp.int32, (RANK, LANES), 1)

    def step(t, carry):
        half = t // SUB
        off = lax.rem(t, SUB) * BLOCK
        rows = pl.ds(pl.multiple_of(t * BLOCK, BLOCK), BLOCK)
        d = a_ref[half, rows, :]
        d = pltpu.roll(d, lax.rem(LANES - off, LANES), 1)
        for j in range(BLOCK):
            cols_ref[j] = jnp.broadcast_to(d[:, j : j + 1], (BLOCK, LANES))
        s, low, inv, y = {}, {}, [], []
        for j in range(BLOCK):
            for i in range(j, BLOCK):
                s[i, j] = cols_ref[j, pl.ds(i, SUB, stride=0), :]
        for i in range(BLOCK):
            eye = jnp.where(lane8 == off + i, -1.0, 0.0)
            row = []
            for h in range(2):
                inside = (lane8 >= off) & (lane8 < off + BLOCK) & (half == h)
                row.append(jnp.where(inside, eye, a_ref[h, pl.ds(t * BLOCK + i, SUB, stride=0), :]))
            y.append(row)
        for k in range(BLOCK):
            inv.append(pltpu.reciprocal(s[k, k]))
            for j in range(k + 1, BLOCK):
                low[j, k] = s[j, k] * inv[k]
            for j in range(k + 1, BLOCK):
                for i in range(j, BLOCK):
                    s[i, j] = s[i, j] - low[i, k] * s[j, k]
                for h in range(2):
                    y[j][h] = y[j][h] - low[j, k] * y[k][h]
        for k in range(BLOCK):
            for h in range(2):
                y[k][h] = y[k][h] * inv[k]
        for k in range(BLOCK - 1, -1, -1):
            for h in range(2):
                w_ref[h, k : k + 1, :] = y[k][h][0:1]
            for j in range(k):
                for h in range(2):
                    y[j][h] = y[j][h] - low[k, j] * y[k][h]
        for h in range(2):
            lanes = pl.ds(h * LANES, LANES)
            r1, r2, r3 = split3(a_ref[h, rows, :])
            lhs_ref[:, lanes] = jnp.concatenate([r1, r1, r2, r2, r1, r3], axis=0)
            w1, w2, w3 = split3(w_ref[h])
            rhs_ref[:, lanes] = jnp.concatenate([w1, w2, w1, w2, w3, w1], axis=0)
        change = lax.dot_general(
            lhs_ref[...], rhs_ref[...], (((0,), (0,)), ((), ())), preferred_element_type=jnp.float32
        )
        for h in range(2):
            inside = (lane_n >= off) & (lane_n < off + BLOCK) & (half == h)
            a_ref[h] = jnp.where(inside, 0.0, a_ref[h]) - change[:, h * LANES : (h + 1) * LANES]
        for h in range(2):
            a_ref[h, rows, :] = w_ref[h]
        return carry

    lax.fori_loop(0, RANK // BLOCK, step, 0)


def kernel(
    t_hbm, fb_ref, fc_ref, out_ref,
    t_buf, b_buf, c_buf, b_wide, c_wide, gb, gc, gb_in, gc_in, a_ref, m_out, m_in,
    cols_ref, w_ref, lhs_ref, rhs_ref,
    t_sem, b_send, b_recv, c_send, c_recv, gb_send, gb_recv, gc_send, gc_recv,
    a_send, a_recv, m_send, m_recv,
):
    ja = lax.axis_index("ja")
    ka = lax.axis_index("ka")
    me = ja * GROUP + ka

    def load(n):
        span = pl.ds(n * (ROWS // CHUNKS), ROWS // CHUNKS)
        return pltpu.make_async_copy(t_hbm.at[span], t_buf.at[span], t_sem.at[n])

    for n in range(CHUNKS):
        load(n).start()

    barrier = pltpu.get_barrier_semaphore()

    def greet(d, carry):
        q = lax.rem(me + d, PLANE)
        pl.semaphore_signal(
            barrier, inc=1, device_id={"ja": q // GROUP, "ka": lax.rem(q, GROUP)}, device_id_type=MESH
        )
        return carry

    lax.fori_loop(1, PLANE, greet, 0)
    b_buf[ka] = fb_ref[...].astype(jnp.float32).T.astype(jnp.bfloat16)
    c_buf[ja] = fc_ref[...].astype(jnp.float32).T.astype(jnp.bfloat16)
    pl.semaphore_wait(barrier, PLANE - 1)

    def remote(src, dst, send, recv, device):
        return pltpu.make_async_remote_copy(
            src_ref=src, dst_ref=dst, send_sem=send, recv_sem=recv, device_id=device, device_id_type=MESH
        )

    def b_copy(d):
        return remote(b_buf.at[ka], b_buf.at[ka], b_send.at[d], b_recv.at[d], {"ka": lax.rem(ka + d, GROUP)})

    def c_copy(d):
        return remote(c_buf.at[ja], c_buf.at[ja], c_send.at[d], c_recv.at[d], {"ja": lax.rem(ja + d, GROUP)})

    def b_landed(d):
        slot = lax.rem(ka + GROUP - d, GROUP)
        return remote(b_buf.at[slot], b_buf.at[slot], b_send.at[d], b_recv.at[d], {"ka": slot})

    def c_landed(d):
        slot = lax.rem(ja + GROUP - d, GROUP)
        return remote(c_buf.at[slot], c_buf.at[slot], c_send.at[d], c_recv.at[d], {"ja": slot})

    for d in range(1, GROUP):
        c_copy(d).start()
        b_copy(d).start()

    for d in range(1, GROUP):
        b_landed(d).wait_recv()
    bt = b_buf[...].reshape(RANK, DEPTH)
    nt = (((1,), (1,)), ((), ()))
    gram = lax.dot_general(bt, bt, nt, preferred_element_type=jnp.float32)
    for h in range(2):
        gb[pl.ds(h * 32, 32)] = gram[:, h * LANES : (h + 1) * LANES].reshape(32, SUB, LANES)

    def gb_copy(d):
        q = lax.rem(ja + d, GROUP)
        return remote(gb.at[q * GROUP + ka], gb_in.at[ja], gb_send.at[d], gb_recv.at[d], {"ja": q})

    def gb_landed(d):
        q = lax.rem(ja + GROUP - d, GROUP)
        return remote(gb.at[q * GROUP + ka], gb_in.at[q], gb_send.at[d], gb_recv.at[d], {"ja": q})

    for d in range(1, GROUP):
        gb_copy(d).start()
    gb_in[ja] = gb[ja * GROUP + ka]

    for d in range(1, GROUP):
        c_landed(d).wait_recv()
    ct = c_buf[...].reshape(RANK, DEPTH)
    gram = lax.dot_general(ct, ct, nt, preferred_element_type=jnp.float32)
    for h in range(2):
        gc[pl.ds(h * 32, 32)] = gram[:, h * LANES : (h + 1) * LANES].reshape(32, SUB, LANES)

    def gc_copy(d):
        q = lax.rem(ka + d, GROUP)
        return remote(gc.at[ja * GROUP + q], gc_in.at[ka], gc_send.at[d], gc_recv.at[d], {"ka": q})

    def gc_landed(d):
        q = lax.rem(ka + GROUP - d, GROUP)
        return remote(gc.at[ja * GROUP + q], gc_in.at[q], gc_send.at[d], gc_recv.at[d], {"ka": q})

    for d in range(1, GROUP):
        gc_copy(d).start()
    gc_in[ka] = gc[ja * GROUP + ka]

    b_wide[...] = bt.astype(jnp.float32).T
    c_wide[...] = ct.astype(jnp.float32).T.astype(jnp.bfloat16)

    def contract(n, carry):
        x = t_buf[pl.ds(n * STEP, STEP)].reshape(STEP * DEPTH, DEPTH)
        inner = jnp.dot(x, c_wide[...], preferred_element_type=jnp.float32)
        total = jnp.sum(inner.reshape(STEP, DEPTH, RANK) * b_wide[...][None], axis=1)
        left, right = total[:, :LANES], total[:, LANES:]
        m_out[2 * n] = jnp.concatenate([left[:4], right[:4]], axis=0)
        m_out[2 * n + 1] = jnp.concatenate([left[4:], right[4:]], axis=0)
        return carry

    steps = ROWS // STEP
    per_chunk = steps // CHUNKS
    for n in range(CHUNKS // 2):
        load(n).wait()
        lax.fori_loop(n * per_chunk, (n + 1) * per_chunk, contract, 0)

    for d in range(1, GROUP):
        gb_landed(d).wait_recv()
        gc_landed(d).wait_recv()
    sum_b = jnp.sum(gb_in[...], axis=0)
    sum_c = jnp.sum(gc_in[...], axis=0)
    my_half = me // 32
    my_row = lax.rem(me, 32) * SUB
    row = lax.broadcasted_iota(jnp.int32, (SUB, LANES), 0) + my_row
    col = lax.broadcasted_iota(jnp.int32, (SUB, LANES), 1) + my_half * LANES
    mine = pl.ds(pl.multiple_of(my_row, SUB), SUB)
    a_ref[my_half, mine, :] = sum_b * sum_c + jnp.where(row == col, RIDGE, 0.0)

    def place(q):
        return {"ja": q // GROUP, "ka": lax.rem(q, GROUP)}

    def tile(q):
        return a_ref.at[q // 32, pl.ds(pl.multiple_of(lax.rem(q, 32) * SUB, SUB), SUB), :]

    def a_copy(d):
        return remote(tile(me), tile(me), a_send.at[d], a_recv.at[d], place(lax.rem(me + d, PLANE)))

    def a_landed(d):
        q = lax.rem(me + PLANE - d, PLANE)
        return remote(tile(q), tile(q), a_send.at[d], a_recv.at[d], place(q))

    def m_copy(d):
        q = lax.rem(me + d, PLANE)
        return remote(m_out.at[q], m_in.at[me], m_send.at[d], m_recv.at[d], place(q))

    def m_landed(d):
        q = lax.rem(me + PLANE - d, PLANE)
        return remote(m_out.at[q], m_in.at[q], m_send.at[d], m_recv.at[d], place(q))

    def each(action):
        def body(d, carry):
            action(d)
            return carry

        lax.fori_loop(1, PLANE, body, 0)

    each(lambda d: a_copy(d).start())
    for n in range(CHUNKS // 2, CHUNKS):
        load(n).wait()
        lax.fori_loop(n * per_chunk, (n + 1) * per_chunk, contract, 0)
    each(lambda d: a_landed(d).wait_recv())
    each(lambda d: m_copy(d).start())
    each(lambda d: a_copy(d).wait_send())
    m_in[me] = m_out[me]

    eliminate(a_ref, cols_ref, w_ref, lhs_ref, rhs_ref)

    each(lambda d: m_landed(d).wait_recv())
    total = jnp.sum(m_in[...], axis=0)
    left, right = total[:4], total[4:]
    for h in range(2):
        part = jnp.dot(left, a_ref[h, pl.ds(0, LANES), :], precision=lax.Precision.HIGHEST,
                       preferred_element_type=jnp.float32)
        part += jnp.dot(right, a_ref[h, pl.ds(LANES, LANES), :], precision=lax.Precision.HIGHEST,
                        preferred_element_type=jnp.float32)
        out_ref[:, h * LANES : (h + 1) * LANES] = -part

    for d in range(1, GROUP):
        b_copy(d).wait_send()
        c_copy(d).wait_send()
        gb_copy(d).wait_send()
        gc_copy(d).wait_send()
    each(lambda d: m_copy(d).wait_send())


def body(tensor, factor_b, factor_c):
    f32, bf16 = jnp.float32, jnp.bfloat16
    vmem, dma = pltpu.VMEM, pltpu.SemaphoreType.DMA
    return pl.pallas_call(
        kernel,
        out_shape=jax.ShapeDtypeStruct((4, RANK), f32),
        in_specs=[
            pl.BlockSpec(memory_space=pl.ANY),
            pl.BlockSpec(memory_space=pltpu.VMEM),
            pl.BlockSpec(memory_space=pltpu.VMEM),
        ],
        out_specs=pl.BlockSpec(memory_space=pltpu.VMEM),
        scratch_shapes=[
            vmem((ROWS, DEPTH, DEPTH), bf16),
            vmem((GROUP, RANK // GROUP, DEPTH), bf16),
            vmem((GROUP, RANK // GROUP, DEPTH), bf16),
            vmem((DEPTH, RANK), f32),
            vmem((DEPTH, RANK), bf16),
            vmem((PLANE, SUB, LANES), f32),
            vmem((PLANE, SUB, LANES), f32),
            vmem((GROUP, SUB, LANES), f32),
            vmem((GROUP, SUB, LANES), f32),
            vmem((2, RANK, LANES), f32),
            vmem((PLANE, SUB, LANES), f32),
            vmem((PLANE, SUB, LANES), f32),
            vmem((BLOCK, BLOCK, LANES), f32),
            vmem((2, BLOCK, LANES), f32),
            vmem((6 * BLOCK, RANK), bf16),
            vmem((6 * BLOCK, RANK), bf16),
            dma((CHUNKS,)),
            *[dma((GROUP,)) for _ in range(8)],
            *[dma((PLANE,)) for _ in range(4)],
        ],
        compiler_params=pltpu.CompilerParams(collective_id=0, has_side_effects=True),
        name="factor_update",
    )(tensor, factor_b, factor_c)


def solution(mesh):
    return jax.shard_map(
        body,
        mesh=mesh,
        in_specs=(P("ia", "ja", "ka"), P("ja", "ka"), P("ka", "ja")),
        out_specs=P(("ia", "ja", "ka"), None),
        check_vma=False,
    )
```

```python
import jax
import jax.numpy as jnp
from jax import lax
from jax.experimental import pallas as pl
from jax.experimental.pallas import tpu as pltpu
from jax.sharding import PartitionSpec as P

MESH = pl.DeviceIdType.MESH
RIDGE = 0.1
GROUP = 8
PLANE = GROUP * GROUP
RANK = 256
LANES = 128
SUB = 8
BLOCK = 16
ROWS = 256
DEPTH = 128
STEP = 8
CHUNKS = 8


def split3(x):
    a = x.astype(jnp.bfloat16)
    rest = x - a.astype(jnp.float32)
    b = rest.astype(jnp.bfloat16)
    c = (rest - b.astype(jnp.float32)).astype(jnp.bfloat16)
    return a, b, c


def eliminate(first, last, a_ref, cols_ref, w_ref, lhs_ref, rhs_ref):
    lane8 = lax.broadcasted_iota(jnp.int32, (SUB, LANES), 1)
    lane_n = lax.broadcasted_iota(jnp.int32, (RANK, LANES), 1)

    def step(t, carry):
        half = t // SUB
        off = lax.rem(t, SUB) * BLOCK
        rows = pl.ds(pl.multiple_of(t * BLOCK, BLOCK), BLOCK)
        d = a_ref[half, rows, :]
        d = pltpu.roll(d, lax.rem(LANES - off, LANES), 1)
        for j in range(BLOCK):
            cols_ref[j] = jnp.broadcast_to(d[:, j : j + 1], (BLOCK, LANES))
        s, low, inv, y = {}, {}, [], []
        for j in range(BLOCK):
            for i in range(j, BLOCK):
                s[i, j] = cols_ref[j, pl.ds(i, SUB, stride=0), :]
        for i in range(BLOCK):
            eye = jnp.where(lane8 == off + i, -1.0, 0.0)
            row = []
            for h in range(2):
                inside = (lane8 >= off) & (lane8 < off + BLOCK) & (half == h)
                row.append(jnp.where(inside, eye, a_ref[h, pl.ds(t * BLOCK + i, SUB, stride=0), :]))
            y.append(row)
        for k in range(BLOCK):
            inv.append(pltpu.reciprocal(s[k, k]))
            for j in range(k + 1, BLOCK):
                low[j, k] = s[j, k] * inv[k]
            for j in range(k + 1, BLOCK):
                for i in range(j, BLOCK):
                    s[i, j] = s[i, j] - low[i, k] * s[j, k]
                for h in range(2):
                    y[j][h] = y[j][h] - low[j, k] * y[k][h]
        for k in range(BLOCK):
            for h in range(2):
                y[k][h] = y[k][h] * inv[k]
        for k in range(BLOCK - 1, -1, -1):
            for h in range(2):
                w_ref[h, k : k + 1, :] = y[k][h][0:1]
            for j in range(k):
                for h in range(2):
                    y[j][h] = y[j][h] - low[k, j] * y[k][h]
        for h in range(2):
            lanes = pl.ds(h * LANES, LANES)
            r1, r2, r3 = split3(a_ref[h, rows, :])
            lhs_ref[:, lanes] = jnp.concatenate([r1, r1, r2, r2, r1, r3], axis=0)
            w1, w2, w3 = split3(w_ref[h])
            rhs_ref[:, lanes] = jnp.concatenate([w1, w2, w1, w2, w3, w1], axis=0)
        change = lax.dot_general(
            lhs_ref[...], rhs_ref[...], (((0,), (0,)), ((), ())), preferred_element_type=jnp.float32
        )
        for h in range(2):
            inside = (lane_n >= off) & (lane_n < off + BLOCK) & (half == h)
            a_ref[h] = jnp.where(inside, 0.0, a_ref[h]) - change[:, h * LANES : (h + 1) * LANES]
        for h in range(2):
            a_ref[h, rows, :] = w_ref[h]
        return carry

    lax.fori_loop(first, last, step, 0)


def kernel(
    t_hbm, fb_hbm, fc_hbm, out_ref,
    t_buf, b_buf, c_buf, b_wide, c_wide, gb, gc, gb_in, gc_in, a_ref, m_out, my_in, mz_out, mz_in,
    cols_ref, w_ref, lhs_ref, rhs_ref,
    f_sem, t_sem, b_send, b_recv, c_send, c_recv, gb_send, gb_recv, gc_send, gc_recv,
    az_send, az_recv, ay_send, ay_recv, my_send, my_recv, mz_send, mz_recv,
):
    ja = lax.axis_index("ja")
    ka = lax.axis_index("ka")
    y, core, z = lax.rem(ja, 4), lax.rem(ka, 2), (ja // 4) * 4 + ka // 2
    column = y * 2 + core

    def along_z(p):
        return {"ja": (p // 4) * 4 + y, "ka": lax.rem(p, 4) * 2 + core}

    def along_y(p):
        return {"ja": (ja // 4) * 4 + p // 2, "ka": (ka // 2) * 2 + lax.rem(p, 2)}

    def tile_of(j, k):
        return (lax.rem(j, 4) * 2 + lax.rem(k, 2)) * GROUP + (j // 4) * 4 + k // 2

    me = tile_of(ja, ka)

    def load(n):
        span = pl.ds(n * (ROWS // CHUNKS), ROWS // CHUNKS)
        return pltpu.make_async_copy(t_hbm.at[span], t_buf.at[span], t_sem.at[n])

    load_b = pltpu.make_async_copy(fb_hbm, b_buf.at[ka], f_sem.at[0])
    load_c = pltpu.make_async_copy(fc_hbm, c_buf.at[ja], f_sem.at[1])
    load_b.start()
    load_c.start()
    for n in range(CHUNKS):
        load(n).start()

    barrier = pltpu.get_barrier_semaphore()

    partners = [{"ja": lax.rem(ja + d, GROUP)} for d in range(1, GROUP)]
    partners += [{"ka": lax.rem(ka + d, GROUP)} for d in range(1, GROUP)]
    partners += [{"ja": lax.rem(ja + 4, GROUP), "ka": lax.rem(ka + 2 * d, GROUP)} for d in range(1, 4)]
    other = ka + 1 - 2 * core
    partners += [{"ja": (ja // 4) * 4 + lax.rem(y + d, 4), "ka": other} for d in range(1, 4)]
    for partner in partners:
        pl.semaphore_signal(barrier, inc=1, device_id=partner, device_id_type=MESH)
    load_b.wait()
    load_c.wait()
    pl.semaphore_wait(barrier, len(partners))

    def remote(src, dst, send, recv, device):
        return pltpu.make_async_remote_copy(
            src_ref=src, dst_ref=dst, send_sem=send, recv_sem=recv, device_id=device, device_id_type=MESH
        )

    def b_copy(d):
        return remote(b_buf.at[ka], b_buf.at[ka], b_send.at[d], b_recv.at[d], {"ka": lax.rem(ka + d, GROUP)})

    def c_copy(d):
        return remote(c_buf.at[ja], c_buf.at[ja], c_send.at[d], c_recv.at[d], {"ja": lax.rem(ja + d, GROUP)})

    def b_landed(d):
        slot = lax.rem(ka + GROUP - d, GROUP)
        return remote(b_buf.at[slot], b_buf.at[slot], b_send.at[d], b_recv.at[d], {"ka": slot})

    def c_landed(d):
        slot = lax.rem(ja + GROUP - d, GROUP)
        return remote(c_buf.at[slot], c_buf.at[slot], c_send.at[d], c_recv.at[d], {"ja": slot})

    for d in range(1, GROUP):
        c_copy(d).start()
        b_copy(d).start()

    for d in range(1, GROUP):
        b_landed(d).wait_recv()
    bt = b_buf[...].reshape(RANK, DEPTH)
    nt = (((1,), (1,)), ((), ()))
    gram = lax.dot_general(bt, bt, nt, preferred_element_type=jnp.float32)
    for h in range(2):
        gb[pl.ds(h * 32, 32)] = gram[:, h * LANES : (h + 1) * LANES].reshape(32, SUB, LANES)

    def gb_copy(d):
        q = lax.rem(ja + d, GROUP)
        return remote(gb.at[tile_of(q, ka)], gb_in.at[ja], gb_send.at[d], gb_recv.at[d], {"ja": q})

    def gb_landed(d):
        q = lax.rem(ja + GROUP - d, GROUP)
        return remote(gb.at[tile_of(q, ka)], gb_in.at[q], gb_send.at[d], gb_recv.at[d], {"ja": q})

    for d in range(1, GROUP):
        gb_copy(d).start()
    gb_in[ja] = gb[me]

    for d in range(1, GROUP):
        c_landed(d).wait_recv()
    ct = c_buf[...].reshape(RANK, DEPTH)
    gram = lax.dot_general(ct, ct, nt, preferred_element_type=jnp.float32)
    for h in range(2):
        gc[pl.ds(h * 32, 32)] = gram[:, h * LANES : (h + 1) * LANES].reshape(32, SUB, LANES)

    def gc_copy(d):
        q = lax.rem(ka + d, GROUP)
        return remote(gc.at[tile_of(ja, q)], gc_in.at[ka], gc_send.at[d], gc_recv.at[d], {"ka": q})

    def gc_landed(d):
        q = lax.rem(ka + GROUP - d, GROUP)
        return remote(gc.at[tile_of(ja, q)], gc_in.at[q], gc_send.at[d], gc_recv.at[d], {"ka": q})

    for d in range(1, GROUP):
        gc_copy(d).start()
    gc_in[ka] = gc[me]

    b_wide[...] = bt.astype(jnp.float32).T
    c_wide[...] = ct.astype(jnp.float32).T.astype(jnp.bfloat16)

    def contract(n, carry):
        x = t_buf[pl.ds(n * STEP, STEP)].reshape(STEP * DEPTH, DEPTH)
        inner = jnp.dot(x, c_wide[...], preferred_element_type=jnp.float32)
        total = jnp.sum(inner.reshape(STEP, DEPTH, RANK) * b_wide[...][None], axis=1)
        left, right = total[:, :LANES], total[:, LANES:]
        j, k = n // 4, lax.rem(n, 4) * 2
        m_out[tile_of(j, k)] = jnp.concatenate([left[:4], right[:4]], axis=0)
        m_out[tile_of(j, k + 1)] = jnp.concatenate([left[4:], right[4:]], axis=0)
        return carry

    steps = ROWS // STEP
    per_chunk = steps // CHUNKS
    for n in range(CHUNKS // 2):
        load(n).wait()
        lax.fori_loop(n * per_chunk, (n + 1) * per_chunk, contract, 0)

    for d in range(1, GROUP):
        gb_landed(d).wait_recv()
        gc_landed(d).wait_recv()
    sum_b = jnp.sum(gb_in[...], axis=0)
    sum_c = jnp.sum(gc_in[...], axis=0)
    my_half = me // 32
    my_row = lax.rem(me, 32) * SUB
    row = lax.broadcasted_iota(jnp.int32, (SUB, LANES), 0) + my_row
    col = lax.broadcasted_iota(jnp.int32, (SUB, LANES), 1) + my_half * LANES
    mine = pl.ds(pl.multiple_of(my_row, SUB), SUB)
    a_ref[my_half, mine, :] = sum_b * sum_c + jnp.where(row == col, RIDGE, 0.0)

    def part(ref, p):
        return ref.at[p // 4, pl.ds(pl.multiple_of(lax.rem(p, 4) * 64, 64), 64), :]

    def az_tile(p):
        start = lax.rem(column, 4) * 64 + p * SUB
        return a_ref.at[column // 4, pl.ds(pl.multiple_of(start, SUB), SUB), :]

    def az_copy(d):
        return remote(az_tile(z), az_tile(z), az_send.at[d], az_recv.at[d], along_z(lax.rem(z + d, GROUP)))

    def az_landed(d):
        p = lax.rem(z + GROUP - d, GROUP)
        return remote(az_tile(p), az_tile(p), az_send.at[d], az_recv.at[d], along_z(p))

    def ay_copy(d):
        return remote(
            part(a_ref, column), part(a_ref, column), ay_send.at[d], ay_recv.at[d], along_y(lax.rem(column + d, GROUP))
        )

    def ay_landed(d):
        p = lax.rem(column + GROUP - d, GROUP)
        return remote(part(a_ref, p), part(a_ref, p), ay_send.at[d], ay_recv.at[d], along_y(p))

    def my_copy(d):
        p = lax.rem(column + d, GROUP)
        return remote(
            m_out.at[pl.ds(p * GROUP, GROUP)], my_in.at[column], my_send.at[d], my_recv.at[d], along_y(p)
        )

    def my_landed(d):
        p = lax.rem(column + GROUP - d, GROUP)
        return remote(m_out.at[pl.ds(p * GROUP, GROUP)], my_in.at[p], my_send.at[d], my_recv.at[d], along_y(p))

    def mz_copy(d):
        p = lax.rem(z + d, GROUP)
        return remote(mz_out.at[p], mz_in.at[z], mz_send.at[d], mz_recv.at[d], along_z(p))

    def mz_landed(d):
        p = lax.rem(z + GROUP - d, GROUP)
        return remote(mz_out.at[p], mz_in.at[p], mz_send.at[d], mz_recv.at[d], along_z(p))

    others = range(1, GROUP)
    for d in others:
        az_copy(d).start()
    for n in range(CHUNKS // 2, CHUNKS):
        load(n).wait()
        lax.fori_loop(n * per_chunk, (n + 1) * per_chunk, contract, 0)
    for d in others:
        az_landed(d).wait_recv()
    for d in others:
        ay_copy(d).start()
    for d in others:
        my_copy(d).start()
    my_in[column] = m_out[pl.ds(column * GROUP, GROUP)]
    for d in others:
        ay_landed(d).wait_recv()
    for d in others:
        az_copy(d).wait_send()
        ay_copy(d).wait_send()

    blocks = RANK // BLOCK
    eliminate(0, blocks // 2, a_ref, cols_ref, w_ref, lhs_ref, rhs_ref)
    for d in others:
        my_landed(d).wait_recv()
    mz_out[...] = jnp.sum(my_in[...], axis=0)
    for d in others:
        mz_copy(d).start()
    mz_in[z] = mz_out[z]
    eliminate(blocks // 2, blocks, a_ref, cols_ref, w_ref, lhs_ref, rhs_ref)
    for d in others:
        mz_landed(d).wait_recv()
    total = jnp.sum(mz_in[...], axis=0)
    left, right = total[:4], total[4:]
    for h in range(2):
        part = jnp.dot(left, a_ref[h, pl.ds(0, LANES), :], precision=lax.Precision.HIGHEST,
                       preferred_element_type=jnp.float32)
        part += jnp.dot(right, a_ref[h, pl.ds(LANES, LANES), :], precision=lax.Precision.HIGHEST,
                        preferred_element_type=jnp.float32)
        out_ref[:, h * LANES : (h + 1) * LANES] = -part

    for d in range(1, GROUP):
        b_copy(d).wait_send()
        c_copy(d).wait_send()
        gb_copy(d).wait_send()
        gc_copy(d).wait_send()
        my_copy(d).wait_send()
        mz_copy(d).wait_send()


def body(tensor, factor_b, factor_c):
    f32, bf16 = jnp.float32, jnp.bfloat16
    vmem, dma = pltpu.VMEM, pltpu.SemaphoreType.DMA
    return pl.pallas_call(
        kernel,
        out_shape=jax.ShapeDtypeStruct((4, RANK), f32),
        in_specs=[
            pl.BlockSpec(memory_space=pl.ANY),
            pl.BlockSpec(memory_space=pl.ANY),
            pl.BlockSpec(memory_space=pl.ANY),
        ],
        out_specs=pl.BlockSpec(memory_space=pltpu.VMEM),
        scratch_shapes=[
            vmem((ROWS, DEPTH, DEPTH), bf16),
            vmem((GROUP, RANK // GROUP, DEPTH), bf16),
            vmem((GROUP, RANK // GROUP, DEPTH), bf16),
            vmem((DEPTH, RANK), f32),
            vmem((DEPTH, RANK), bf16),
            vmem((PLANE, SUB, LANES), f32),
            vmem((PLANE, SUB, LANES), f32),
            vmem((GROUP, SUB, LANES), f32),
            vmem((GROUP, SUB, LANES), f32),
            vmem((2, RANK, LANES), f32),
            vmem((PLANE, SUB, LANES), f32),
            vmem((GROUP, GROUP, SUB, LANES), f32),
            vmem((GROUP, SUB, LANES), f32),
            vmem((GROUP, SUB, LANES), f32),
            vmem((BLOCK, BLOCK, LANES), f32),
            vmem((2, BLOCK, LANES), f32),
            vmem((6 * BLOCK, RANK), bf16),
            vmem((6 * BLOCK, RANK), bf16),
            dma((2,)),
            dma((CHUNKS,)),
            *[dma((GROUP,)) for _ in range(16)],
        ],
        compiler_params=pltpu.CompilerParams(collective_id=0, has_side_effects=True),
        name="factor_update",
    )(tensor, factor_b.T, factor_c.T)


def solution(mesh):
    return jax.shard_map(
        body,
        mesh=mesh,
        in_specs=(P("ia", "ja", "ka"), P("ja", "ka"), P("ka", "ja")),
        out_specs=P(("ia", "ja", "ka"), None),
        check_vma=False,
    )
```

```python
import jax
import jax.numpy as jnp
from jax import lax
from jax.experimental import pallas as pl
from jax.experimental.pallas import tpu as pltpu
from jax.sharding import PartitionSpec as P

MESH = pl.DeviceIdType.MESH
RIDGE = 0.1
GROUP = 8
PLANE = GROUP * GROUP
RANK = 256
LANES = 128
SUB = 8
PIV = 8
HALF = LANES // PIV
ROWS = 256
DEPTH = 128
STEP = 8
CHUNKS = 8


def split3(x):
    a = x.astype(jnp.bfloat16)
    rest = x - a.astype(jnp.float32)
    b = rest.astype(jnp.bfloat16)
    c = (rest - b.astype(jnp.float32)).astype(jnp.bfloat16)
    return a, b, c


def lane(x, idx):
    return jnp.take_along_axis(x, jnp.broadcast_to(idx, x.shape), axis=1)

def start_sweep(a_ref, next_ref, w_ref, lhs_ref, rhs_ref):
    lhs_ref[...] = jnp.zeros_like(lhs_ref)
    rhs_ref[...] = jnp.zeros_like(rhs_ref)
    for h in range(2):
        next_ref[h] = a_ref[h, pl.ds(0, PIV), :]
        w_ref[h] = a_ref[h, pl.ds(0, PIV), :]


def trail(t, a_ref, w_ref, lhs_ref, rhs_ref):
    lane_n = lax.broadcasted_iota(jnp.int32, (RANK, LANES), 1)
    change = jnp.dot(lhs_ref[...], rhs_ref[...], preferred_element_type=jnp.float32)
    rows = pl.ds(pl.multiple_of(jnp.maximum(t, 0) * PIV, PIV), PIV)
    for h in range(2):
        lo = t * PIV - h * LANES
        inside = (lane_n >= lo) & (lane_n < lo + PIV)
        a_ref[h] = jnp.where(inside, 0.0, a_ref[h]) - change[:, h * LANES : (h + 1) * LANES]
    for h in range(2):
        a_ref[h, rows, :] = w_ref[h]


def sweep(first, last, a_ref, next_ref, w_ref, lhs_ref, rhs_ref):
    lane8 = lax.broadcasted_iota(jnp.int32, (PIV, LANES), 1)
    row8 = lax.broadcasted_iota(jnp.int32, (PIV, LANES), 0)

    def within(t, h):
        lo = t * PIV - h * LANES
        return (lane8 >= lo) & (lane8 < lo + PIV)

    def spread(x, k):
        return jnp.broadcast_to(x[k : k + 1], (PIV, LANES))

    def less(rows, t, factors, w):
        out = []
        for h in range(2):
            terms = [factors[k] * spread(w[h], k) for k in range(PIV)]
            while len(terms) > 1:
                terms = [p + q for p, q in zip(terms[::2], terms[1::2])]
            out.append(jnp.where(within(t, h), 0.0, rows[h]) - terms[0])
        return out

    def step(t, carry):
        half, off = t // HALF, lax.rem(t, HALF) * PIV
        here = [next_ref[0], next_ref[1]]
        d = jnp.where(half == 0, here[0], here[1])
        s = [lane(d, off + j) for j in range(PIV)]
        before = t - 1
        ahead = pl.ds(pl.multiple_of(lax.rem(t + 1, RANK // PIV) * PIV, PIV), PIV)
        base = [a_ref[h, ahead, :] for h in range(2)]
        old = jnp.where(before < HALF, base[0], base[1])
        old_off = lax.rem(before + HALF, HALF) * PIV
        factors = [jnp.where(t > 0, lane(old, old_off + k), 0.0) for k in range(PIV)]
        base = less(base, before, factors, [w_ref[0], w_ref[1]])
        c = jnp.where(half == 0, base[0], base[1])
        factors = [lane(c, off + k) for k in range(PIV)]
        trail(before, a_ref, w_ref, lhs_ref, rhs_ref)
        for h in range(2):
            r1, r2, r3 = split3(here[h])
            lhs_ref[h * LANES : (h + 1) * LANES, :] = jnp.concatenate([r1, r1, r2, r2, r1, r3], axis=0).T
        y = []
        for h in range(2):
            eye = jnp.where(lane8 == t * PIV - h * LANES + row8, -1.0, 0.0)
            y.append(jnp.where(within(t, h), eye, here[h]))
        scale = None
        for k in range(PIV):
            inv = pltpu.reciprocal(spread(s[k], k))
            scale = inv if k == 0 else jnp.where(row8 == k, inv, scale)
            away = jnp.where(row8 == k, 0.0, s[k])
            m = away * inv
            for j in range(k + 1, PIV):
                if j == k + 1:
                    s[j] = s[j] - (away * spread(s[j], k)) * inv
                else:
                    s[j] = s[j] - m * spread(s[j], k)
            for h in range(2):
                y[h] = y[h] - m * spread(y[h], k)
        w = [y[h] * scale for h in range(2)]
        after = less(base, t, factors, w)
        for h in range(2):
            next_ref[h] = after[h]
            w_ref[h] = w[h]
            w1, w2, w3 = split3(w[h])
            rhs_ref[:, h * LANES : (h + 1) * LANES] = jnp.concatenate([w1, w2, w1, w2, w3, w1], axis=0)
        return carry

    lax.fori_loop(first, last, step, 0)


def kernel(
    t_hbm, fb_hbm, fc_hbm, out_ref,
    t_buf, b_buf, c_buf, b_wide, c_wide, gb, gc, gb_in, gc_in, a_ref, m_out, my_in, mz_out, mz_in,
    next_ref, w_ref, lhs_ref, rhs_ref,
    f_sem, t_sem, b_send, b_recv, c_send, c_recv, gb_send, gb_recv, gc_send, gc_recv,
    az_send, az_recv, ay_send, ay_recv, my_send, my_recv, mz_send, mz_recv,
):
    ja = lax.axis_index("ja")
    ka = lax.axis_index("ka")
    y, core, z = lax.rem(ja, 4), lax.rem(ka, 2), (ja // 4) * 4 + ka // 2
    column = y * 2 + core

    def along_z(p):
        return {"ja": (p // 4) * 4 + y, "ka": lax.rem(p, 4) * 2 + core}

    def along_y(p):
        return {"ja": (ja // 4) * 4 + p // 2, "ka": (ka // 2) * 2 + lax.rem(p, 2)}

    def tile_of(j, k):
        return (lax.rem(j, 4) * 2 + lax.rem(k, 2)) * GROUP + (j // 4) * 4 + k // 2

    me = tile_of(ja, ka)

    def load(n):
        span = pl.ds(n * (ROWS // CHUNKS), ROWS // CHUNKS)
        return pltpu.make_async_copy(t_hbm.at[span], t_buf.at[span], t_sem.at[n])

    load_b = pltpu.make_async_copy(fb_hbm, b_buf.at[ka], f_sem.at[0])
    load_c = pltpu.make_async_copy(fc_hbm, c_buf.at[ja], f_sem.at[1])
    load_b.start()
    load_c.start()
    for n in range(CHUNKS):
        load(n).start()

    barrier = pltpu.get_barrier_semaphore()

    partners = [{"ja": lax.rem(ja + d, GROUP)} for d in range(1, GROUP)]
    partners += [{"ka": lax.rem(ka + d, GROUP)} for d in range(1, GROUP)]
    partners += [{"ja": lax.rem(ja + 4, GROUP), "ka": lax.rem(ka + 2 * d, GROUP)} for d in range(1, 4)]
    other = ka + 1 - 2 * core
    partners += [{"ja": (ja // 4) * 4 + lax.rem(y + d, 4), "ka": other} for d in range(1, 4)]
    for partner in partners:
        pl.semaphore_signal(barrier, inc=1, device_id=partner, device_id_type=MESH)
    load_b.wait()
    load_c.wait()
    pl.semaphore_wait(barrier, len(partners))

    def remote(src, dst, send, recv, device):
        return pltpu.make_async_remote_copy(
            src_ref=src, dst_ref=dst, send_sem=send, recv_sem=recv, device_id=device, device_id_type=MESH
        )

    def b_copy(d):
        return remote(b_buf.at[ka], b_buf.at[ka], b_send.at[d], b_recv.at[d], {"ka": lax.rem(ka + d, GROUP)})

    def c_copy(d):
        return remote(c_buf.at[ja], c_buf.at[ja], c_send.at[d], c_recv.at[d], {"ja": lax.rem(ja + d, GROUP)})

    def b_landed(d):
        slot = lax.rem(ka + GROUP - d, GROUP)
        return remote(b_buf.at[slot], b_buf.at[slot], b_send.at[d], b_recv.at[d], {"ka": slot})

    def c_landed(d):
        slot = lax.rem(ja + GROUP - d, GROUP)
        return remote(c_buf.at[slot], c_buf.at[slot], c_send.at[d], c_recv.at[d], {"ja": slot})

    for d in range(1, GROUP):
        c_copy(d).start()
        b_copy(d).start()

    for d in range(1, GROUP):
        b_landed(d).wait_recv()
    bt = b_buf[...].reshape(RANK, DEPTH)
    nt = (((1,), (1,)), ((), ()))
    gram = lax.dot_general(bt, bt, nt, preferred_element_type=jnp.float32)
    for h in range(2):
        gb[pl.ds(h * 32, 32)] = gram[:, h * LANES : (h + 1) * LANES].reshape(32, SUB, LANES)

    def gb_copy(d):
        q = lax.rem(ja + d, GROUP)
        return remote(gb.at[tile_of(q, ka)], gb_in.at[ja], gb_send.at[d], gb_recv.at[d], {"ja": q})

    def gb_landed(d):
        q = lax.rem(ja + GROUP - d, GROUP)
        return remote(gb.at[tile_of(q, ka)], gb_in.at[q], gb_send.at[d], gb_recv.at[d], {"ja": q})

    for d in range(1, GROUP):
        gb_copy(d).start()
    gb_in[ja] = gb[me]

    for d in range(1, GROUP):
        c_landed(d).wait_recv()
    ct = c_buf[...].reshape(RANK, DEPTH)
    gram = lax.dot_general(ct, ct, nt, preferred_element_type=jnp.float32)
    for h in range(2):
        gc[pl.ds(h * 32, 32)] = gram[:, h * LANES : (h + 1) * LANES].reshape(32, SUB, LANES)

    def gc_copy(d):
        q = lax.rem(ka + d, GROUP)
        return remote(gc.at[tile_of(ja, q)], gc_in.at[ka], gc_send.at[d], gc_recv.at[d], {"ka": q})

    def gc_landed(d):
        q = lax.rem(ka + GROUP - d, GROUP)
        return remote(gc.at[tile_of(ja, q)], gc_in.at[q], gc_send.at[d], gc_recv.at[d], {"ka": q})

    for d in range(1, GROUP):
        gc_copy(d).start()
    gc_in[ka] = gc[me]

    b_wide[...] = bt.astype(jnp.float32).T
    c_wide[...] = ct.astype(jnp.float32).T.astype(jnp.bfloat16)

    def contract(n, carry):
        x = t_buf[pl.ds(n * STEP, STEP)].reshape(STEP * DEPTH, DEPTH)
        inner = jnp.dot(x, c_wide[...], preferred_element_type=jnp.float32)
        total = jnp.sum(inner.reshape(STEP, DEPTH, RANK) * b_wide[...][None], axis=1)
        left, right = total[:, :LANES], total[:, LANES:]
        j, k = n // 4, lax.rem(n, 4) * 2
        m_out[tile_of(j, k)] = jnp.concatenate([left[:4], right[:4]], axis=0)
        m_out[tile_of(j, k + 1)] = jnp.concatenate([left[4:], right[4:]], axis=0)
        return carry

    per_chunk = ROWS // STEP // CHUNKS

    def contract_chunks(first, last):
        for n in range(first, last):
            load(n).wait()
        lax.fori_loop(first * per_chunk, last * per_chunk, contract, 0)

    contract_chunks(0, 3)

    for d in range(1, GROUP):
        gb_landed(d).wait_recv()
        gc_landed(d).wait_recv()
    sum_b = jnp.sum(gb_in[...], axis=0)
    sum_c = jnp.sum(gc_in[...], axis=0)
    my_half = me // 32
    my_row = lax.rem(me, 32) * SUB
    row = lax.broadcasted_iota(jnp.int32, (SUB, LANES), 0) + my_row
    col = lax.broadcasted_iota(jnp.int32, (SUB, LANES), 1) + my_half * LANES
    mine = pl.ds(pl.multiple_of(my_row, SUB), SUB)
    a_ref[my_half, mine, :] = sum_b * sum_c + jnp.where(row == col, RIDGE, 0.0)

    def part(ref, p):
        return ref.at[p // 4, pl.ds(pl.multiple_of(lax.rem(p, 4) * 64, 64), 64), :]

    def az_tile(p):
        start = lax.rem(column, 4) * 64 + p * SUB
        return a_ref.at[column // 4, pl.ds(pl.multiple_of(start, SUB), SUB), :]

    def az_copy(d):
        return remote(az_tile(z), az_tile(z), az_send.at[d], az_recv.at[d], along_z(lax.rem(z + d, GROUP)))

    def az_landed(d):
        p = lax.rem(z + GROUP - d, GROUP)
        return remote(az_tile(p), az_tile(p), az_send.at[d], az_recv.at[d], along_z(p))

    def ay_copy(d):
        return remote(
            part(a_ref, column), part(a_ref, column), ay_send.at[d], ay_recv.at[d], along_y(lax.rem(column + d, GROUP))
        )

    def ay_landed(d):
        p = lax.rem(column + GROUP - d, GROUP)
        return remote(part(a_ref, p), part(a_ref, p), ay_send.at[d], ay_recv.at[d], along_y(p))

    def my_copy(d):
        p = lax.rem(column + d, GROUP)
        return remote(
            m_out.at[pl.ds(p * GROUP, GROUP)], my_in.at[column], my_send.at[d], my_recv.at[d], along_y(p)
        )

    def my_landed(d):
        p = lax.rem(column + GROUP - d, GROUP)
        return remote(m_out.at[pl.ds(p * GROUP, GROUP)], my_in.at[p], my_send.at[d], my_recv.at[d], along_y(p))

    def mz_copy(d):
        p = lax.rem(z + d, GROUP)
        return remote(mz_out.at[p], mz_in.at[z], mz_send.at[d], mz_recv.at[d], along_z(p))

    def mz_landed(d):
        p = lax.rem(z + GROUP - d, GROUP)
        return remote(mz_out.at[p], mz_in.at[p], mz_send.at[d], mz_recv.at[d], along_z(p))

    others = range(1, GROUP)
    for d in others:
        az_copy(d).start()
    contract_chunks(3, 5)
    for d in others:
        az_landed(d).wait_recv()
    for d in others:
        ay_copy(d).start()
    contract_chunks(5, CHUNKS)
    for d in others:
        my_copy(d).start()
    my_in[column] = m_out[pl.ds(column * GROUP, GROUP)]
    for d in others:
        ay_landed(d).wait_recv()
    for d in others:
        az_copy(d).wait_send()
        ay_copy(d).wait_send()

    blocks = RANK // PIV
    start_sweep(a_ref, next_ref, w_ref, lhs_ref, rhs_ref)
    sweep(0, blocks // 2, a_ref, next_ref, w_ref, lhs_ref, rhs_ref)
    for d in others:
        my_landed(d).wait_recv()
    mz_out[...] = jnp.sum(my_in[...], axis=0)
    for d in others:
        mz_copy(d).start()
    mz_in[z] = mz_out[z]
    sweep(blocks // 2, blocks, a_ref, next_ref, w_ref, lhs_ref, rhs_ref)
    trail(blocks - 1, a_ref, w_ref, lhs_ref, rhs_ref)
    for d in others:
        mz_landed(d).wait_recv()
    total = jnp.sum(mz_in[...], axis=0)
    left, right = total[:4], total[4:]
    for h in range(2):
        part = jnp.dot(left, a_ref[h, pl.ds(0, LANES), :], precision=lax.Precision.HIGHEST,
                       preferred_element_type=jnp.float32)
        part += jnp.dot(right, a_ref[h, pl.ds(LANES, LANES), :], precision=lax.Precision.HIGHEST,
                        preferred_element_type=jnp.float32)
        out_ref[:, h * LANES : (h + 1) * LANES] = -part

    for d in range(1, GROUP):
        b_copy(d).wait_send()
        c_copy(d).wait_send()
        gb_copy(d).wait_send()
        gc_copy(d).wait_send()
        my_copy(d).wait_send()
        mz_copy(d).wait_send()


def body(tensor, factor_b, factor_c):
    f32, bf16 = jnp.float32, jnp.bfloat16
    vmem, dma = pltpu.VMEM, pltpu.SemaphoreType.DMA
    return pl.pallas_call(
        kernel,
        out_shape=jax.ShapeDtypeStruct((4, RANK), f32),
        in_specs=[
            pl.BlockSpec(memory_space=pl.ANY),
            pl.BlockSpec(memory_space=pl.ANY),
            pl.BlockSpec(memory_space=pl.ANY),
        ],
        out_specs=pl.BlockSpec(memory_space=pltpu.VMEM),
        scratch_shapes=[
            vmem((ROWS, DEPTH, DEPTH), bf16),
            vmem((GROUP, RANK // GROUP, DEPTH), bf16),
            vmem((GROUP, RANK // GROUP, DEPTH), bf16),
            vmem((DEPTH, RANK), f32),
            vmem((DEPTH, RANK), bf16),
            vmem((PLANE, SUB, LANES), f32),
            vmem((PLANE, SUB, LANES), f32),
            vmem((GROUP, SUB, LANES), f32),
            vmem((GROUP, SUB, LANES), f32),
            vmem((2, RANK, LANES), f32),
            vmem((PLANE, SUB, LANES), f32),
            vmem((GROUP, GROUP, SUB, LANES), f32),
            vmem((GROUP, SUB, LANES), f32),
            vmem((GROUP, SUB, LANES), f32),
            vmem((2, PIV, LANES), f32),
            vmem((2, PIV, LANES), f32),
            vmem((RANK, 6 * PIV), bf16),
            vmem((6 * PIV, RANK), bf16),
            dma((2,)),
            dma((CHUNKS,)),
            *[dma((GROUP,)) for _ in range(16)],
        ],
        compiler_params=pltpu.CompilerParams(collective_id=0, has_side_effects=True),
        name="factor_update",
    )(tensor, factor_b.T, factor_c.T)


def solution(mesh):
    return jax.shard_map(
        body,
        mesh=mesh,
        in_specs=(P("ia", "ja", "ka"), P("ja", "ka"), P("ka", "ja")),
        out_specs=P(("ia", "ja", "ka"), None),
        check_vma=False,
    )
```

```python
import jax
import jax.numpy as jnp
from jax import lax
from jax.experimental import pallas as pl
from jax.experimental.pallas import tpu as pltpu
from jax.sharding import PartitionSpec as P

MESH = pl.DeviceIdType.MESH
RIDGE = 0.1
GROUP = 8
PLANE = GROUP * GROUP
RANK = 256
LANES = 128
SUB = 8
PIV = 16
HALF = LANES // PIV
ROWS = 256
DEPTH = 128
STEP = 8
CHUNKS = 8


def split3(x):
    a = x.astype(jnp.bfloat16)
    rest = x - a.astype(jnp.float32)
    b = rest.astype(jnp.bfloat16)
    c = (rest - b.astype(jnp.float32)).astype(jnp.bfloat16)
    return a, b, c


def lane(x, idx):
    return jnp.take_along_axis(x, jnp.broadcast_to(idx, x.shape), axis=1)


def start_sweep(a_ref, next_ref, w_ref, lhs_ref, rhs_ref):
    lhs_ref[...] = jnp.zeros_like(lhs_ref)
    rhs_ref[...] = jnp.zeros_like(rhs_ref)
    for h in range(2):
        next_ref[h] = a_ref[h, pl.ds(0, PIV), :]
        w_ref[h] = a_ref[h, pl.ds(0, PIV), :]


def trail(t, a_ref, w_ref, lhs_ref, rhs_ref):
    lane_n = lax.broadcasted_iota(jnp.int32, (RANK, LANES), 1)
    change = jnp.dot(lhs_ref[...], rhs_ref[...], preferred_element_type=jnp.float32)
    rows = pl.ds(pl.multiple_of(jnp.maximum(t, 0) * PIV, PIV), PIV)
    for h in range(2):
        lo = t * PIV - h * LANES
        inside = (lane_n >= lo) & (lane_n < lo + PIV)
        a_ref[h] = jnp.where(inside, 0.0, a_ref[h]) - change[:, h * LANES : (h + 1) * LANES]
    for h in range(2):
        a_ref[h, rows, :] = w_ref[h]


def sweep(first, last, a_ref, next_ref, w_ref, lhs_ref, rhs_ref):
    lane8 = lax.broadcasted_iota(jnp.int32, (SUB, LANES), 1)
    row8 = lax.broadcasted_iota(jnp.int32, (SUB, LANES), 0)
    lane16 = lax.broadcasted_iota(jnp.int32, (PIV, LANES), 1)
    groups = range(PIV // SUB)

    def spread(x, k):
        return jnp.broadcast_to(x[k // SUB][k % SUB : k % SUB + 1], (SUB, LANES))

    def step(t, carry):
        half, off = t // HALF, lax.rem(t, HALF) * PIV
        here = [[next_ref[h, g * SUB : (g + 1) * SUB, :] for g in groups] for h in range(2)]
        d = [jnp.where(half == 0, here[0][g], here[1][g]) for g in groups]
        s = [[lane(d[g], off + j) for g in groups] for j in range(PIV)]
        ahead = pl.ds(pl.multiple_of(lax.rem(t + 1, RANK // PIV) * PIV, PIV), PIV)
        change = jnp.dot(lhs_ref[ahead, :], rhs_ref[...], preferred_element_type=jnp.float32)
        base = []
        for h in range(2):
            lo = (t - 1) * PIV - h * LANES
            inside = (lane16 >= lo) & (lane16 < lo + PIV)
            base.append(jnp.where(inside, 0.0, a_ref[h, ahead, :]) - change[:, h * LANES : (h + 1) * LANES])
        c = jnp.where(half == 0, base[0], base[1])
        factors = [[lane(c[g * SUB : (g + 1) * SUB], off + k) for k in range(PIV)] for g in groups]
        trail(t - 1, a_ref, w_ref, lhs_ref, rhs_ref)
        for h in range(2):
            r1, r2, r3 = split3(next_ref[h])
            lhs_ref[h * LANES : (h + 1) * LANES, :] = jnp.concatenate([r1, r1, r2, r2, r1, r3], axis=0).T
        y = []
        for h in range(2):
            lo = t * PIV - h * LANES
            inside = (lane8 >= lo) & (lane8 < lo + PIV)
            y.append([
                jnp.where(inside, jnp.where(lane8 == lo + g * SUB + row8, -1.0, 0.0), here[h][g]) for g in groups
            ])
        scale = [None for _ in groups]
        for k in range(PIV):
            inv = pltpu.reciprocal(spread(s[k], k))
            g0, r0 = k // SUB, k % SUB
            scale[g0] = inv if r0 == 0 else jnp.where(row8 == r0, inv, scale[g0])
            away = [jnp.where(row8 == r0, 0.0, s[k][g]) if g == g0 else s[k][g] for g in groups]
            m = [away[g] * inv for g in groups]
            for j in range(k + 1, PIV):
                sj = spread(s[j], k)
                if j == k + 1:
                    s[j] = [s[j][g] - (away[g] * sj) * inv for g in groups]
                else:
                    s[j] = [s[j][g] - m[g] * sj for g in groups]
            for h in range(2):
                yk = spread(y[h], k)
                y[h] = [y[h][g] - m[g] * yk for g in groups]
        w = [[y[h][g] * scale[g] for g in groups] for h in range(2)]
        for g in groups:
            for h in range(2):
                terms = [factors[g][k] * spread(w[h], k) for k in range(PIV)]
                while len(terms) > 1:
                    terms = [p + q for p, q in zip(terms[::2], terms[1::2])]
                lo = t * PIV - h * LANES
                inside = (lane8 >= lo) & (lane8 < lo + PIV)
                next_ref[h, g * SUB : (g + 1) * SUB, :] = jnp.where(inside, 0.0, base[h][g * SUB : (g + 1) * SUB]) - terms[0]
        for h in range(2):
            full = jnp.concatenate(w[h], axis=0)
            w_ref[h] = full
            w1, w2, w3 = split3(full)
            rhs_ref[:, h * LANES : (h + 1) * LANES] = jnp.concatenate([w1, w2, w1, w2, w3, w1], axis=0)
        return carry

    lax.fori_loop(first, last, step, 0)


def kernel(
    t_hbm, fb_hbm, fc_hbm, out_ref,
    t_buf, b_buf, c_buf, b_wide, c_wide, gb, gc, gb_in, gc_in, a_ref, m_out, my_in, mz_out, mz_in,
    next_ref, w_ref, lhs_ref, rhs_ref,
    f_sem, t_sem, b_send, b_recv, c_send, c_recv, gb_send, gb_recv, gc_send, gc_recv,
    az_send, az_recv, ay_send, ay_recv, my_send, my_recv, mz_send, mz_recv,
):
    ja = lax.axis_index("ja")
    ka = lax.axis_index("ka")
    y, core, z = lax.rem(ja, 4), lax.rem(ka, 2), (ja // 4) * 4 + ka // 2
    column = y * 2 + core

    def along_z(p):
        return {"ja": (p // 4) * 4 + y, "ka": lax.rem(p, 4) * 2 + core}

    def along_y(p):
        return {"ja": (ja // 4) * 4 + p // 2, "ka": (ka // 2) * 2 + lax.rem(p, 2)}

    def tile_of(j, k):
        return (lax.rem(j, 4) * 2 + lax.rem(k, 2)) * GROUP + (j // 4) * 4 + k // 2

    me = tile_of(ja, ka)

    def load(n):
        span = pl.ds(n * (ROWS // CHUNKS), ROWS // CHUNKS)
        return pltpu.make_async_copy(t_hbm.at[span], t_buf.at[span], t_sem.at[n])

    load_b = pltpu.make_async_copy(fb_hbm, b_buf.at[ka], f_sem.at[0])
    load_c = pltpu.make_async_copy(fc_hbm, c_buf.at[ja], f_sem.at[1])
    load_b.start()
    load_c.start()
    order = [lax.rem(y + d, 4) + 4 * e for d in (2, 1, 3, 0) for e in range(2)]
    for n in order:
        load(n).start()

    barrier = pltpu.get_barrier_semaphore()

    partners = [{"ja": lax.rem(ja + d, GROUP)} for d in range(1, GROUP)]
    partners += [{"ka": lax.rem(ka + d, GROUP)} for d in range(1, GROUP)]
    partners += [{"ja": lax.rem(ja + 4, GROUP), "ka": lax.rem(ka + 2 * d, GROUP)} for d in range(1, 4)]
    other = ka + 1 - 2 * core
    partners += [{"ja": (ja // 4) * 4 + lax.rem(y + d, 4), "ka": other} for d in range(1, 4)]
    for partner in partners:
        pl.semaphore_signal(barrier, inc=1, device_id=partner, device_id_type=MESH)
    load_b.wait()
    load_c.wait()
    pl.semaphore_wait(barrier, len(partners))

    def remote(src, dst, send, recv, device):
        return pltpu.make_async_remote_copy(
            src_ref=src, dst_ref=dst, send_sem=send, recv_sem=recv, device_id=device, device_id_type=MESH
        )

    def b_copy(d):
        return remote(b_buf.at[ka], b_buf.at[ka], b_send.at[d], b_recv.at[d], {"ka": lax.rem(ka + d, GROUP)})

    def c_copy(d):
        return remote(c_buf.at[ja], c_buf.at[ja], c_send.at[d], c_recv.at[d], {"ja": lax.rem(ja + d, GROUP)})

    def b_landed(d):
        slot = lax.rem(ka + GROUP - d, GROUP)
        return remote(b_buf.at[slot], b_buf.at[slot], b_send.at[d], b_recv.at[d], {"ka": slot})

    def c_landed(d):
        slot = lax.rem(ja + GROUP - d, GROUP)
        return remote(c_buf.at[slot], c_buf.at[slot], c_send.at[d], c_recv.at[d], {"ja": slot})

    for d in range(1, GROUP):
        c_copy(d).start()
        b_copy(d).start()

    for d in range(1, GROUP):
        b_landed(d).wait_recv()
    bt = b_buf[...].reshape(RANK, DEPTH)
    nt = (((1,), (1,)), ((), ()))
    gram = lax.dot_general(bt, bt, nt, preferred_element_type=jnp.float32)
    for h in range(2):
        gb[pl.ds(h * 32, 32)] = gram[:, h * LANES : (h + 1) * LANES].reshape(32, SUB, LANES)

    def gb_copy(d):
        q = lax.rem(ja + d, GROUP)
        return remote(gb.at[tile_of(q, ka)], gb_in.at[ja], gb_send.at[d], gb_recv.at[d], {"ja": q})

    def gb_landed(d):
        q = lax.rem(ja + GROUP - d, GROUP)
        return remote(gb.at[tile_of(q, ka)], gb_in.at[q], gb_send.at[d], gb_recv.at[d], {"ja": q})

    for d in range(1, GROUP):
        gb_copy(d).start()
    gb_in[ja] = gb[me]

    for d in range(1, GROUP):
        c_landed(d).wait_recv()
    ct = c_buf[...].reshape(RANK, DEPTH)
    gram = lax.dot_general(ct, ct, nt, preferred_element_type=jnp.float32)
    for h in range(2):
        gc[pl.ds(h * 32, 32)] = gram[:, h * LANES : (h + 1) * LANES].reshape(32, SUB, LANES)

    def gc_copy(d):
        q = lax.rem(ka + d, GROUP)
        return remote(gc.at[tile_of(ja, q)], gc_in.at[ka], gc_send.at[d], gc_recv.at[d], {"ka": q})

    def gc_landed(d):
        q = lax.rem(ka + GROUP - d, GROUP)
        return remote(gc.at[tile_of(ja, q)], gc_in.at[q], gc_send.at[d], gc_recv.at[d], {"ka": q})

    for d in range(1, GROUP):
        gc_copy(d).start()
    gc_in[ka] = gc[me]

    b_wide[...] = bt.astype(jnp.float32).T
    c_wide[...] = ct.astype(jnp.float32).T.astype(jnp.bfloat16)

    def contract(n, carry):
        x = t_buf[pl.ds(n * STEP, STEP)].reshape(STEP * DEPTH, DEPTH)
        inner = jnp.dot(x, c_wide[...], preferred_element_type=jnp.float32)
        total = jnp.sum(inner.reshape(STEP, DEPTH, RANK) * b_wide[...][None], axis=1)
        left, right = total[:, :LANES], total[:, LANES:]
        j, k = n // 4, lax.rem(n, 4) * 2
        m_out[tile_of(j, k)] = jnp.concatenate([left[:4], right[:4]], axis=0)
        m_out[tile_of(j, k + 1)] = jnp.concatenate([left[4:], right[4:]], axis=0)
        return carry

    per_chunk = ROWS // STEP // CHUNKS

    def contract_chunk(n):
        load(n).wait()
        lax.fori_loop(0, per_chunk, lambda i, carry: contract(n * per_chunk + i, carry), 0)

    def my_column(dy, e):
        return lax.rem(y + dy, 4) * 2 + (core if e == 0 else 1 - core)

    def my_copy(dy, e):
        p, k = my_column(dy, e), dy * 2 + e
        return remote(
            m_out.at[pl.ds(p * GROUP, GROUP)], my_in.at[column], my_send.at[k], my_recv.at[k], along_y(p)
        )

    def my_landed(dy, e):
        p, k = my_column(4 - dy, e), dy * 2 + e
        return remote(m_out.at[pl.ds(p * GROUP, GROUP)], my_in.at[p], my_send.at[k], my_recv.at[k], along_y(p))

    my_all = [(dy, e) for dy in range(4) for e in range(2) if dy + e > 0]

    contract_chunk(order[0])
    contract_chunk(order[1])
    my_copy(2, 0).start()
    my_copy(2, 1).start()
    contract_chunk(order[2])

    for d in range(1, GROUP):
        gb_landed(d).wait_recv()
        gc_landed(d).wait_recv()
    sum_b = jnp.sum(gb_in[...], axis=0)
    sum_c = jnp.sum(gc_in[...], axis=0)
    my_half = me // 32
    my_row = lax.rem(me, 32) * SUB
    row = lax.broadcasted_iota(jnp.int32, (SUB, LANES), 0) + my_row
    col = lax.broadcasted_iota(jnp.int32, (SUB, LANES), 1) + my_half * LANES
    mine = pl.ds(pl.multiple_of(my_row, SUB), SUB)
    a_ref[my_half, mine, :] = sum_b * sum_c + jnp.where(row == col, RIDGE, 0.0)

    def part(ref, p):
        return ref.at[p // 4, pl.ds(pl.multiple_of(lax.rem(p, 4) * 64, 64), 64), :]

    def az_tile(p):
        start = lax.rem(column, 4) * 64 + p * SUB
        return a_ref.at[column // 4, pl.ds(pl.multiple_of(start, SUB), SUB), :]

    def az_copy(d):
        return remote(az_tile(z), az_tile(z), az_send.at[d], az_recv.at[d], along_z(lax.rem(z + d, GROUP)))

    def az_landed(d):
        p = lax.rem(z + GROUP - d, GROUP)
        return remote(az_tile(p), az_tile(p), az_send.at[d], az_recv.at[d], along_z(p))

    def ay_copy(d):
        return remote(
            part(a_ref, column), part(a_ref, column), ay_send.at[d], ay_recv.at[d], along_y(lax.rem(column + d, GROUP))
        )

    def ay_landed(d):
        p = lax.rem(column + GROUP - d, GROUP)
        return remote(part(a_ref, p), part(a_ref, p), ay_send.at[d], ay_recv.at[d], along_y(p))

    def mz_copy(d):
        p = lax.rem(z + d, GROUP)
        return remote(mz_out.at[p], mz_in.at[z], mz_send.at[d], mz_recv.at[d], along_z(p))

    def mz_landed(d):
        p = lax.rem(z + GROUP - d, GROUP)
        return remote(mz_out.at[p], mz_in.at[p], mz_send.at[d], mz_recv.at[d], along_z(p))

    others = range(1, GROUP)
    for d in others:
        az_copy(d).start()
    contract_chunk(order[3])
    my_copy(1, 0).start()
    my_copy(1, 1).start()
    contract_chunk(order[4])
    contract_chunk(order[5])
    my_copy(3, 0).start()
    my_copy(3, 1).start()
    for d in others:
        az_landed(d).wait_recv()
    for d in others:
        ay_copy(d).start()
    contract_chunk(order[6])
    contract_chunk(order[7])
    my_copy(0, 1).start()
    my_in[column] = m_out[pl.ds(column * GROUP, GROUP)]
    for d in others:
        ay_landed(d).wait_recv()
    for d in others:
        az_copy(d).wait_send()
        ay_copy(d).wait_send()

    blocks = RANK // PIV
    start_sweep(a_ref, next_ref, w_ref, lhs_ref, rhs_ref)
    sweep(0, 4, a_ref, next_ref, w_ref, lhs_ref, rhs_ref)
    for dy, e in my_all:
        my_landed(dy, e).wait_recv()
    mz_out[...] = jnp.sum(my_in[...], axis=0)
    for d in others:
        mz_copy(d).start()
    mz_in[z] = mz_out[z]
    sweep(4, blocks, a_ref, next_ref, w_ref, lhs_ref, rhs_ref)
    trail(blocks - 1, a_ref, w_ref, lhs_ref, rhs_ref)
    for d in others:
        mz_landed(d).wait_recv()
    total = jnp.sum(mz_in[...], axis=0)
    left, right = total[:4], total[4:]
    for h in range(2):
        part = jnp.dot(left, a_ref[h, pl.ds(0, LANES), :], precision=lax.Precision.HIGHEST,
                       preferred_element_type=jnp.float32)
        part += jnp.dot(right, a_ref[h, pl.ds(LANES, LANES), :], precision=lax.Precision.HIGHEST,
                        preferred_element_type=jnp.float32)
        out_ref[:, h * LANES : (h + 1) * LANES] = -part

    for d in range(1, GROUP):
        b_copy(d).wait_send()
        c_copy(d).wait_send()
        gb_copy(d).wait_send()
        gc_copy(d).wait_send()
        mz_copy(d).wait_send()
    for dy, e in my_all:
        my_copy(dy, e).wait_send()


def body(tensor, factor_b, factor_c):
    f32, bf16 = jnp.float32, jnp.bfloat16
    vmem, dma = pltpu.VMEM, pltpu.SemaphoreType.DMA
    return pl.pallas_call(
        kernel,
        out_shape=jax.ShapeDtypeStruct((4, RANK), f32),
        in_specs=[
            pl.BlockSpec(memory_space=pl.ANY),
            pl.BlockSpec(memory_space=pl.ANY),
            pl.BlockSpec(memory_space=pl.ANY),
        ],
        out_specs=pl.BlockSpec(memory_space=pltpu.VMEM),
        scratch_shapes=[
            vmem((ROWS, DEPTH, DEPTH), bf16),
            vmem((GROUP, RANK // GROUP, DEPTH), bf16),
            vmem((GROUP, RANK // GROUP, DEPTH), bf16),
            vmem((DEPTH, RANK), f32),
            vmem((DEPTH, RANK), bf16),
            vmem((PLANE, SUB, LANES), f32),
            vmem((PLANE, SUB, LANES), f32),
            vmem((GROUP, SUB, LANES), f32),
            vmem((GROUP, SUB, LANES), f32),
            vmem((2, RANK, LANES), f32),
            vmem((PLANE, SUB, LANES), f32),
            vmem((GROUP, GROUP, SUB, LANES), f32),
            vmem((GROUP, SUB, LANES), f32),
            vmem((GROUP, SUB, LANES), f32),
            vmem((2, PIV, LANES), f32),
            vmem((2, PIV, LANES), f32),
            vmem((RANK, 6 * PIV), bf16),
            vmem((6 * PIV, RANK), bf16),
            dma((2,)),
            dma((CHUNKS,)),
            *[dma((GROUP,)) for _ in range(16)],
        ],
        compiler_params=pltpu.CompilerParams(collective_id=0, has_side_effects=True),
        name="factor_update",
    )(tensor, factor_b.T, factor_c.T)


def solution(mesh):
    return jax.shard_map(
        body,
        mesh=mesh,
        in_specs=(P("ia", "ja", "ka"), P("ja", "ka"), P("ka", "ja")),
        out_specs=P(("ia", "ja", "ka"), None),
        check_vma=False,
    )
```

```python
import jax
import jax.numpy as jnp
from jax import lax
from jax.experimental import pallas as pl
from jax.experimental.pallas import tpu as pltpu
from jax.sharding import PartitionSpec as P

MESH = pl.DeviceIdType.MESH
RIDGE = 0.1
GROUP = 8
PLANE = GROUP * GROUP
RANK = 256
LANES = 128
SUB = 8
PIV = 16
HALF = LANES // PIV
ROWS = 256
DEPTH = 128
STEP = 8
CHUNKS = 8


def split3(x):
    a = x.astype(jnp.bfloat16)
    rest = x - a.astype(jnp.float32)
    b = rest.astype(jnp.bfloat16)
    c = (rest - b.astype(jnp.float32)).astype(jnp.bfloat16)
    return a, b, c


def lane(x, idx):
    return jnp.take_along_axis(x, jnp.broadcast_to(idx, x.shape), axis=1)


def start_sweep(a_ref, next_ref, w_ref, lhs_ref, rhs_ref):
    lhs_ref[...] = jnp.zeros_like(lhs_ref)
    rhs_ref[...] = jnp.zeros_like(rhs_ref)
    for h in range(2):
        next_ref[h] = a_ref[h, pl.ds(0, PIV), :]
        w_ref[h] = a_ref[h, pl.ds(0, PIV), :]


def trail(t, a_ref, w_ref, lhs_ref, rhs_ref):
    lane_n = lax.broadcasted_iota(jnp.int32, (RANK, LANES), 1)
    change = jnp.dot(lhs_ref[...], rhs_ref[...], preferred_element_type=jnp.float32)
    rows = pl.ds(pl.multiple_of(jnp.maximum(t, 0) * PIV, PIV), PIV)
    for h in range(2):
        lo = t * PIV - h * LANES
        inside = (lane_n >= lo) & (lane_n < lo + PIV)
        a_ref[h] = jnp.where(inside, 0.0, a_ref[h]) - change[:, h * LANES : (h + 1) * LANES]
    for h in range(2):
        a_ref[h, rows, :] = w_ref[h]


def sweep(first, last, a_ref, next_ref, w_ref, lhs_ref, rhs_ref):
    lane8 = lax.broadcasted_iota(jnp.int32, (SUB, LANES), 1)
    row8 = lax.broadcasted_iota(jnp.int32, (SUB, LANES), 0)
    lane16 = lax.broadcasted_iota(jnp.int32, (PIV, LANES), 1)
    groups = range(PIV // SUB)

    def spread(x, k):
        return jnp.broadcast_to(x[k // SUB][k % SUB : k % SUB + 1], (SUB, LANES))

    def step(t, carry):
        half, off = t // HALF, lax.rem(t, HALF) * PIV
        here = [[next_ref[h, g * SUB : (g + 1) * SUB, :] for g in groups] for h in range(2)]
        d = [jnp.where(half == 0, here[0][g], here[1][g]) for g in groups]
        s = [[lane(d[g], off + j) for g in groups] for j in range(PIV)]
        ahead = pl.ds(pl.multiple_of(lax.rem(t + 1, RANK // PIV) * PIV, PIV), PIV)
        change = jnp.dot(lhs_ref[ahead, :], rhs_ref[...], preferred_element_type=jnp.float32)
        base = []
        for h in range(2):
            lo = (t - 1) * PIV - h * LANES
            inside = (lane16 >= lo) & (lane16 < lo + PIV)
            base.append(jnp.where(inside, 0.0, a_ref[h, ahead, :]) - change[:, h * LANES : (h + 1) * LANES])
        c = jnp.where(half == 0, base[0], base[1])
        factors = [[lane(c[g * SUB : (g + 1) * SUB], off + k) for k in range(PIV)] for g in groups]
        trail(t - 1, a_ref, w_ref, lhs_ref, rhs_ref)
        for h in range(2):
            r1, r2, r3 = split3(next_ref[h])
            lhs_ref[h * LANES : (h + 1) * LANES, :] = jnp.concatenate([r1, r1, r2, r2, r1, r3], axis=0).T
        y = []
        for h in range(2):
            lo = t * PIV - h * LANES
            inside = (lane8 >= lo) & (lane8 < lo + PIV)
            y.append([
                jnp.where(inside, jnp.where(lane8 == lo + g * SUB + row8, -1.0, 0.0), here[h][g]) for g in groups
            ])
        scale = [None for _ in groups]
        for k in range(PIV):
            inv = pltpu.reciprocal(spread(s[k], k))
            g0, r0 = k // SUB, k % SUB
            scale[g0] = inv if r0 == 0 else jnp.where(row8 == r0, inv, scale[g0])
            away = [jnp.where(row8 == r0, 0.0, s[k][g]) if g == g0 else s[k][g] for g in groups]
            m = [away[g] * inv for g in groups]
            for j in range(k + 1, PIV):
                sj = spread(s[j], k)
                if j == k + 1:
                    s[j] = [s[j][g] - (away[g] * sj) * inv for g in groups]
                else:
                    s[j] = [s[j][g] - m[g] * sj for g in groups]
            for h in range(2):
                yk = spread(y[h], k)
                y[h] = [y[h][g] - m[g] * yk for g in groups]
        w = [[y[h][g] * scale[g] for g in groups] for h in range(2)]
        for g in groups:
            for h in range(2):
                terms = [factors[g][k] * spread(w[h], k) for k in range(PIV)]
                while len(terms) > 1:
                    terms = [p + q for p, q in zip(terms[::2], terms[1::2])]
                lo = t * PIV - h * LANES
                inside = (lane8 >= lo) & (lane8 < lo + PIV)
                next_ref[h, g * SUB : (g + 1) * SUB, :] = jnp.where(inside, 0.0, base[h][g * SUB : (g + 1) * SUB]) - terms[0]
        for h in range(2):
            full = jnp.concatenate(w[h], axis=0)
            w_ref[h] = full
            w1, w2, w3 = split3(full)
            rhs_ref[:, h * LANES : (h + 1) * LANES] = jnp.concatenate([w1, w2, w1, w2, w3, w1], axis=0)
        return carry

    lax.fori_loop(first, last, step, 0)


def kernel(
    t_hbm, fb_hbm, fc_hbm, out_ref,
    t_buf, b_buf, c_buf, b_wide, c_wide, gb, gc, gb_in, gc_in, a_ref, m_out, my_in, mz_out, mz_in,
    next_ref, w_ref, lhs_ref, rhs_ref,
    f_sem, t_sem, b_send, b_recv, c_send, c_recv, gb_send, gb_recv, gc_send, gc_recv,
    az_send, az_recv, ay_send, ay_recv, my_send, my_recv, mz_send, mz_recv,
):
    ja = lax.axis_index("ja")
    ka = lax.axis_index("ka")
    y, core, z = lax.rem(ja, 4), lax.rem(ka, 2), (ja // 4) * 4 + ka // 2
    column = y * 2 + core

    def along_z(p):
        return {"ja": (p // 4) * 4 + y, "ka": lax.rem(p, 4) * 2 + core}

    def along_y(p):
        return {"ja": (ja // 4) * 4 + p // 2, "ka": (ka // 2) * 2 + lax.rem(p, 2)}

    def tile_of(j, k):
        return (lax.rem(j, 4) * 2 + lax.rem(k, 2)) * GROUP + (j // 4) * 4 + k // 2

    me = tile_of(ja, ka)

    def load(n):
        span = pl.ds(n * (ROWS // CHUNKS), ROWS // CHUNKS)
        return pltpu.make_async_copy(t_hbm.at[span], t_buf.at[span], t_sem.at[n])

    load_b = pltpu.make_async_copy(fb_hbm, b_buf.at[ka], f_sem.at[0])
    load_c = pltpu.make_async_copy(fc_hbm, c_buf.at[ja], f_sem.at[1])
    load_b.start()
    load_c.start()
    order = [lax.rem(y + d, 4) + 4 * e for d in (2, 1, 3, 0) for e in range(2)]
    for n in order:
        load(n).start()

    barrier = pltpu.get_barrier_semaphore()

    partners = [{"ja": lax.rem(ja + d, GROUP)} for d in range(1, GROUP)]
    partners += [{"ka": lax.rem(ka + d, GROUP)} for d in range(1, GROUP)]
    partners += [{"ja": lax.rem(ja + 4, GROUP), "ka": lax.rem(ka + 2 * d, GROUP)} for d in range(1, 4)]
    other = ka + 1 - 2 * core
    partners += [{"ja": (ja // 4) * 4 + lax.rem(y + d, 4), "ka": other} for d in range(1, 4)]
    for partner in partners:
        pl.semaphore_signal(barrier, inc=1, device_id=partner, device_id_type=MESH)
    load_b.wait()
    load_c.wait()
    pl.semaphore_wait(barrier, len(partners))

    def remote(src, dst, send, recv, device):
        return pltpu.make_async_remote_copy(
            src_ref=src, dst_ref=dst, send_sem=send, recv_sem=recv, device_id=device, device_id_type=MESH
        )

    def b_copy(d):
        return remote(b_buf.at[ka], b_buf.at[ka], b_send.at[d], b_recv.at[d], {"ka": lax.rem(ka + d, GROUP)})

    def c_copy(d):
        return remote(c_buf.at[ja], c_buf.at[ja], c_send.at[d], c_recv.at[d], {"ja": lax.rem(ja + d, GROUP)})

    def b_landed(d):
        slot = lax.rem(ka + GROUP - d, GROUP)
        return remote(b_buf.at[slot], b_buf.at[slot], b_send.at[d], b_recv.at[d], {"ka": slot})

    def c_landed(d):
        slot = lax.rem(ja + GROUP - d, GROUP)
        return remote(c_buf.at[slot], c_buf.at[slot], c_send.at[d], c_recv.at[d], {"ja": slot})

    for d in range(1, GROUP):
        c_copy(d).start()
        b_copy(d).start()

    for d in range(1, GROUP):
        b_landed(d).wait_recv()
    bt = b_buf[...].reshape(RANK, DEPTH)
    nt = (((1,), (1,)), ((), ()))
    gram = lax.dot_general(bt, bt, nt, preferred_element_type=jnp.float32)
    for h in range(2):
        gb[pl.ds(h * 32, 32)] = gram[:, h * LANES : (h + 1) * LANES].reshape(32, SUB, LANES)

    def gb_copy(d):
        q = lax.rem(ja + d, GROUP)
        return remote(gb.at[tile_of(q, ka)], gb_in.at[ja], gb_send.at[d], gb_recv.at[d], {"ja": q})

    def gb_landed(d):
        q = lax.rem(ja + GROUP - d, GROUP)
        return remote(gb.at[tile_of(q, ka)], gb_in.at[q], gb_send.at[d], gb_recv.at[d], {"ja": q})

    for d in range(1, GROUP):
        gb_copy(d).start()
    gb_in[ja] = gb[me]

    for d in range(1, GROUP):
        c_landed(d).wait_recv()
    ct = c_buf[...].reshape(RANK, DEPTH)
    first = lax.rem(y, 2) * 4 + ja // 4
    run = jnp.concatenate([c_buf[first], c_buf[first + 2]], axis=0)
    side = c_buf[pl.ds((y // 2) * 4, 4)].reshape(LANES, DEPTH)
    gram = lax.dot_general(run, side, nt, preferred_element_type=jnp.float32)
    gc[...] = gram.reshape(GROUP, SUB, LANES)

    def gc_copy(d):
        q = lax.rem(ka + d, GROUP)
        return remote(gc.at[lax.rem(q, 2) * 4 + q // 2], gc_in.at[ka], gc_send.at[d], gc_recv.at[d], {"ka": q})

    def gc_landed(d):
        q = lax.rem(ka + GROUP - d, GROUP)
        return remote(gc.at[lax.rem(q, 2) * 4 + q // 2], gc_in.at[q], gc_send.at[d], gc_recv.at[d], {"ka": q})

    for d in range(1, GROUP):
        gc_copy(d).start()
    gc_in[ka] = gc[core * 4 + ka // 2]

    b_wide[...] = bt.astype(jnp.float32).T
    c_wide[...] = ct.astype(jnp.float32).T.astype(jnp.bfloat16)

    def contract(n, carry):
        x = t_buf[pl.ds(n * STEP, STEP)].reshape(STEP * DEPTH, DEPTH)
        inner = jnp.dot(x, c_wide[...], preferred_element_type=jnp.float32)
        total = jnp.sum(inner.reshape(STEP, DEPTH, RANK) * b_wide[...][None], axis=1)
        left, right = total[:, :LANES], total[:, LANES:]
        j, k = n // 4, lax.rem(n, 4) * 2
        m_out[tile_of(j, k)] = jnp.concatenate([left[:4], right[:4]], axis=0)
        m_out[tile_of(j, k + 1)] = jnp.concatenate([left[4:], right[4:]], axis=0)
        return carry

    per_chunk = ROWS // STEP // CHUNKS

    def contract_chunk(n):
        load(n).wait()
        lax.fori_loop(0, per_chunk, lambda i, carry: contract(n * per_chunk + i, carry), 0)

    def my_column(dy, e):
        return lax.rem(y + dy, 4) * 2 + (core if e == 0 else 1 - core)

    def my_copy(dy, e):
        p, k = my_column(dy, e), dy * 2 + e
        return remote(
            m_out.at[pl.ds(p * GROUP, GROUP)], my_in.at[column], my_send.at[k], my_recv.at[k], along_y(p)
        )

    def my_landed(dy, e):
        p, k = my_column(4 - dy, e), dy * 2 + e
        return remote(m_out.at[pl.ds(p * GROUP, GROUP)], my_in.at[p], my_send.at[k], my_recv.at[k], along_y(p))

    my_all = [(dy, e) for dy in range(4) for e in range(2) if dy + e > 0]

    contract_chunk(order[0])
    contract_chunk(order[1])
    my_copy(2, 0).start()
    my_copy(2, 1).start()
    contract_chunk(order[2])

    for d in range(1, GROUP):
        gb_landed(d).wait_recv()
        gc_landed(d).wait_recv()
    sum_b = jnp.sum(gb_in[...], axis=0)
    sum_c = jnp.sum(gc_in[...], axis=0)
    my_half = me // 32
    my_row = lax.rem(me, 32) * SUB
    row = lax.broadcasted_iota(jnp.int32, (SUB, LANES), 0) + my_row
    col = lax.broadcasted_iota(jnp.int32, (SUB, LANES), 1) + my_half * LANES
    mine = pl.ds(pl.multiple_of(my_row, SUB), SUB)
    a_ref[my_half, mine, :] = sum_b * sum_c + jnp.where(row == col, RIDGE, 0.0)

    def rows_of(p, q, count):
        start = lax.rem(p, 4) * 64 + q * SUB
        return a_ref.at[p // 4, pl.ds(pl.multiple_of(start, SUB), count * SUB), :]

    def z_at(e, d):
        return lax.rem(z // 4 + e, 2) * 4 + lax.rem(z + d, 4)

    def az_copy(e, d):
        tile, k = rows_of(column, z, 1), e * 4 + d
        return remote(tile, tile, az_send.at[k], az_recv.at[k], along_z(z_at(e, d)))

    def az_landed(e, d):
        q, k = z_at(e, 4 - d), e * 4 + d
        tile = rows_of(column, q, 1)
        return remote(tile, tile, az_send.at[k], az_recv.at[k], along_z(q))

    def ay_copy(e, d):
        tiles = rows_of(column, lax.rem(z // 4 + e, 2) * 4, 4)
        return remote(tiles, tiles, ay_send.at[e, d], ay_recv.at[e, d], along_y(lax.rem(column + d, GROUP)))

    def ay_landed(e, d):
        p = lax.rem(column + GROUP - d, GROUP)
        tiles = rows_of(p, lax.rem(z // 4 + e, 2) * 4, 4)
        return remote(tiles, tiles, ay_send.at[e, d], ay_recv.at[e, d], along_y(p))

    def mz_copy(d):
        p = lax.rem(z + d, GROUP)
        return remote(mz_out.at[p], mz_in.at[z], mz_send.at[d], mz_recv.at[d], along_z(p))

    def mz_landed(d):
        p = lax.rem(z + GROUP - d, GROUP)
        return remote(mz_out.at[p], mz_in.at[p], mz_send.at[d], mz_recv.at[d], along_z(p))

    others = range(1, GROUP)
    az_all = [(e, d) for e in (1, 0) for d in range(4) if e + d > 0]

    def pass_on(e):
        for d in range(4):
            if e + d > 0:
                az_landed(e, d).wait_recv()
        for d in others:
            ay_copy(e, d).start()

    for e, d in az_all:
        az_copy(e, d).start()
    contract_chunk(order[3])
    my_copy(1, 0).start()
    my_copy(1, 1).start()
    contract_chunk(order[4])
    pass_on(0)
    contract_chunk(order[5])
    pass_on(1)
    my_copy(3, 0).start()
    my_copy(3, 1).start()
    contract_chunk(order[6])
    contract_chunk(order[7])
    my_copy(0, 1).start()
    my_in[column] = m_out[pl.ds(column * GROUP, GROUP)]
    for d in others:
        for e in range(2):
            ay_landed(e, d).wait_recv()
    for d in others:
        for e in range(2):
            ay_copy(e, d).wait_send()
    for e, d in az_all:
        az_copy(e, d).wait_send()

    blocks = RANK // PIV
    start_sweep(a_ref, next_ref, w_ref, lhs_ref, rhs_ref)
    sweep(0, 4, a_ref, next_ref, w_ref, lhs_ref, rhs_ref)
    for dy, e in my_all:
        my_landed(dy, e).wait_recv()
    mz_out[...] = jnp.sum(my_in[...], axis=0)
    for d in others:
        mz_copy(d).start()
    mz_in[z] = mz_out[z]
    sweep(4, blocks, a_ref, next_ref, w_ref, lhs_ref, rhs_ref)
    trail(blocks - 1, a_ref, w_ref, lhs_ref, rhs_ref)
    for d in others:
        mz_landed(d).wait_recv()
    total = jnp.sum(mz_in[...], axis=0)
    left, right = total[:4], total[4:]
    for h in range(2):
        part = jnp.dot(left, a_ref[h, pl.ds(0, LANES), :], precision=lax.Precision.HIGHEST,
                       preferred_element_type=jnp.float32)
        part += jnp.dot(right, a_ref[h, pl.ds(LANES, LANES), :], precision=lax.Precision.HIGHEST,
                        preferred_element_type=jnp.float32)
        out_ref[:, h * LANES : (h + 1) * LANES] = -part

    for d in range(1, GROUP):
        b_copy(d).wait_send()
        c_copy(d).wait_send()
        gb_copy(d).wait_send()
        gc_copy(d).wait_send()
        mz_copy(d).wait_send()
    for dy, e in my_all:
        my_copy(dy, e).wait_send()


def body(tensor, factor_b, factor_c):
    f32, bf16 = jnp.float32, jnp.bfloat16
    vmem, dma = pltpu.VMEM, pltpu.SemaphoreType.DMA
    return pl.pallas_call(
        kernel,
        out_shape=jax.ShapeDtypeStruct((4, RANK), f32),
        in_specs=[
            pl.BlockSpec(memory_space=pl.ANY),
            pl.BlockSpec(memory_space=pl.ANY),
            pl.BlockSpec(memory_space=pl.ANY),
        ],
        out_specs=pl.BlockSpec(memory_space=pltpu.VMEM),
        scratch_shapes=[
            vmem((ROWS, DEPTH, DEPTH), bf16),
            vmem((GROUP, RANK // GROUP, DEPTH), bf16),
            vmem((GROUP, RANK // GROUP, DEPTH), bf16),
            vmem((DEPTH, RANK), f32),
            vmem((DEPTH, RANK), bf16),
            vmem((PLANE, SUB, LANES), f32),
            vmem((GROUP, SUB, LANES), f32),
            vmem((GROUP, SUB, LANES), f32),
            vmem((GROUP, SUB, LANES), f32),
            vmem((2, RANK, LANES), f32),
            vmem((PLANE, SUB, LANES), f32),
            vmem((GROUP, GROUP, SUB, LANES), f32),
            vmem((GROUP, SUB, LANES), f32),
            vmem((GROUP, SUB, LANES), f32),
            vmem((2, PIV, LANES), f32),
            vmem((2, PIV, LANES), f32),
            vmem((RANK, 6 * PIV), bf16),
            vmem((6 * PIV, RANK), bf16),
            dma((2,)),
            dma((CHUNKS,)),
            *[dma((GROUP,)) for _ in range(10)],
            *[dma((2, GROUP)) for _ in range(2)],
            *[dma((GROUP,)) for _ in range(4)],
        ],
        compiler_params=pltpu.CompilerParams(collective_id=0, has_side_effects=True),
        name="factor_update",
    )(tensor, factor_b.T, factor_c.T)


def solution(mesh):
    return jax.shard_map(
        body,
        mesh=mesh,
        in_specs=(P("ia", "ja", "ka"), P("ja", "ka"), P("ka", "ja")),
        out_specs=P(("ia", "ja", "ka"), None),
        check_vma=False,
    )
```

```python
import jax
import jax.numpy as jnp
from jax import lax
from jax.experimental import pallas as pl
from jax.experimental.pallas import tpu as pltpu
from jax.sharding import PartitionSpec as P

MESH = pl.DeviceIdType.MESH
RIDGE = 0.1
GROUP = 8
PLANE = GROUP * GROUP
RANK = 256
LANES = 128
SUB = 8
PIV = 16
HALF = LANES // PIV
ROWS = 256
DEPTH = 128
STEP = 8
CHUNKS = 8


def split3(x):
    a = x.astype(jnp.bfloat16)
    rest = x - a.astype(jnp.float32)
    b = rest.astype(jnp.bfloat16)
    c = (rest - b.astype(jnp.float32)).astype(jnp.bfloat16)
    return a, b, c


def lane(x, idx):
    return jnp.take_along_axis(x, jnp.broadcast_to(idx, x.shape), axis=1)


def start_sweep(a_ref, next_ref, w_ref, lhs_ref, rhs_ref):
    lhs_ref[...] = jnp.zeros_like(lhs_ref)
    rhs_ref[...] = jnp.zeros_like(rhs_ref)
    for h in range(2):
        next_ref[h] = a_ref[h, pl.ds(0, PIV), :]
        w_ref[h] = a_ref[h, pl.ds(0, PIV), :]


def trail(t, a_ref, w_ref, lhs_ref, rhs_ref):
    lane_n = lax.broadcasted_iota(jnp.int32, (RANK, LANES), 1)
    change = jnp.dot(lhs_ref[...], rhs_ref[...], preferred_element_type=jnp.float32)
    rows = pl.ds(pl.multiple_of(jnp.maximum(t, 0) * PIV, PIV), PIV)
    for h in range(2):
        lo = t * PIV - h * LANES
        inside = (lane_n >= lo) & (lane_n < lo + PIV)
        a_ref[h] = jnp.where(inside, 0.0, a_ref[h]) - change[:, h * LANES : (h + 1) * LANES]
    for h in range(2):
        a_ref[h, rows, :] = w_ref[h]


def sweep(first, last, a_ref, next_ref, w_ref, lhs_ref, rhs_ref):
    lane8 = lax.broadcasted_iota(jnp.int32, (SUB, LANES), 1)
    row8 = lax.broadcasted_iota(jnp.int32, (SUB, LANES), 0)
    lane16 = lax.broadcasted_iota(jnp.int32, (PIV, LANES), 1)
    groups = range(PIV // SUB)

    def spread(x, k):
        return jnp.broadcast_to(x[k // SUB][k % SUB : k % SUB + 1], (SUB, LANES))

    def step(t, carry):
        half, off = t // HALF, lax.rem(t, HALF) * PIV
        here = [[next_ref[h, g * SUB : (g + 1) * SUB, :] for g in groups] for h in range(2)]
        d = [jnp.where(half == 0, here[0][g], here[1][g]) for g in groups]
        s = [[lane(d[g], off + j) for g in groups] for j in range(PIV)]
        ahead = pl.ds(pl.multiple_of(lax.rem(t + 1, RANK // PIV) * PIV, PIV), PIV)
        change = jnp.dot(lhs_ref[ahead, :], rhs_ref[...], preferred_element_type=jnp.float32)
        base = []
        for h in range(2):
            lo = (t - 1) * PIV - h * LANES
            inside = (lane16 >= lo) & (lane16 < lo + PIV)
            base.append(jnp.where(inside, 0.0, a_ref[h, ahead, :]) - change[:, h * LANES : (h + 1) * LANES])
        c = jnp.where(half == 0, base[0], base[1])
        factors = [[lane(c[g * SUB : (g + 1) * SUB], off + k) for k in range(PIV)] for g in groups]
        trail(t - 1, a_ref, w_ref, lhs_ref, rhs_ref)
        for h in range(2):
            r1, r2, r3 = split3(next_ref[h])
            lhs_ref[h * LANES : (h + 1) * LANES, :] = jnp.concatenate([r1, r1, r2, r2, r1, r3], axis=0).T
        y = []
        for h in range(2):
            lo = t * PIV - h * LANES
            inside = (lane8 >= lo) & (lane8 < lo + PIV)
            y.append([
                jnp.where(inside, jnp.where(lane8 == lo + g * SUB + row8, -1.0, 0.0), here[h][g]) for g in groups
            ])
        scale = [None for _ in groups]
        for k in range(PIV):
            inv = pltpu.reciprocal(spread(s[k], k))
            g0, r0 = k // SUB, k % SUB
            scale[g0] = inv if r0 == 0 else jnp.where(row8 == r0, inv, scale[g0])
            away = [jnp.where(row8 == r0, 0.0, s[k][g]) if g == g0 else s[k][g] for g in groups]
            m = [away[g] * inv for g in groups]
            for j in range(k + 1, PIV):
                sj = spread(s[j], k)
                if j == k + 1:
                    s[j] = [s[j][g] - (away[g] * sj) * inv for g in groups]
                else:
                    s[j] = [s[j][g] - m[g] * sj for g in groups]
            for h in range(2):
                yk = spread(y[h], k)
                y[h] = [y[h][g] - m[g] * yk for g in groups]
        w = [[y[h][g] * scale[g] for g in groups] for h in range(2)]
        for g in groups:
            for h in range(2):
                terms = [factors[g][k] * spread(w[h], k) for k in range(PIV)]
                while len(terms) > 1:
                    terms = [p + q for p, q in zip(terms[::2], terms[1::2])]
                lo = t * PIV - h * LANES
                inside = (lane8 >= lo) & (lane8 < lo + PIV)
                next_ref[h, g * SUB : (g + 1) * SUB, :] = jnp.where(inside, 0.0, base[h][g * SUB : (g + 1) * SUB]) - terms[0]
        for h in range(2):
            full = jnp.concatenate(w[h], axis=0)
            w_ref[h] = full
            w1, w2, w3 = split3(full)
            rhs_ref[:, h * LANES : (h + 1) * LANES] = jnp.concatenate([w1, w2, w1, w2, w3, w1], axis=0)
        return carry

    lax.fori_loop(first, last, step, 0)


def kernel(
    t_hbm, fb_hbm, fc_hbm, out_ref,
    t_buf, b_buf, c_buf, b_wide, c_wide, gb, gc, gb_in, gc_in, a_ref, m_out, my_in, mz_out, mz_in,
    next_ref, w_ref, lhs_ref, rhs_ref,
    f_sem, t_sem, b_send, b_recv, c_send, c_recv, gb_send, gb_recv, gc_send, gc_recv,
    az_send, az_recv, ay_send, ay_recv, my_send, my_recv, mz_send, mz_recv,
):
    ja = lax.axis_index("ja")
    ka = lax.axis_index("ka")
    y, core, z = lax.rem(ja, 4), lax.rem(ka, 2), (ja // 4) * 4 + ka // 2
    column = y * 2 + core

    def along_z(p):
        return {"ja": (p // 4) * 4 + y, "ka": lax.rem(p, 4) * 2 + core}

    def along_y(p):
        return {"ja": (ja // 4) * 4 + p // 2, "ka": (ka // 2) * 2 + lax.rem(p, 2)}

    def tile_of(j, k):
        return (lax.rem(j, 4) * 2 + lax.rem(k, 2)) * GROUP + (j // 4) * 4 + k // 2

    me = tile_of(ja, ka)

    def load(n):
        span = pl.ds(n * (ROWS // CHUNKS), ROWS // CHUNKS)
        return pltpu.make_async_copy(t_hbm.at[span], t_buf.at[span], t_sem.at[n])

    load_b = pltpu.make_async_copy(fb_hbm, b_buf.at[ka], f_sem.at[0])
    load_c = pltpu.make_async_copy(fc_hbm, c_buf.at[ja], f_sem.at[1])
    load_b.start()
    load_c.start()
    order = [lax.rem(y + d, 4) + 4 * e for d in (2, 1, 3, 0) for e in range(2)]
    for n in order:
        load(n).start()

    barrier = pltpu.get_barrier_semaphore()

    partners = [{"ja": lax.rem(ja + d, GROUP)} for d in range(1, GROUP)]
    partners += [{"ka": lax.rem(ka + d, GROUP)} for d in range(1, GROUP)]
    partners += [{"ja": lax.rem(ja + 4, GROUP), "ka": lax.rem(ka + 2 * d, GROUP)} for d in range(1, 4)]
    other = ka + 1 - 2 * core
    partners += [{"ja": (ja // 4) * 4 + lax.rem(y + d, 4), "ka": other} for d in range(1, 4)]
    for partner in partners:
        pl.semaphore_signal(barrier, inc=1, device_id=partner, device_id_type=MESH)
    load_b.wait()
    load_c.wait()
    pl.semaphore_wait(barrier, len(partners))

    def remote(src, dst, send, recv, device):
        return pltpu.make_async_remote_copy(
            src_ref=src, dst_ref=dst, send_sem=send, recv_sem=recv, device_id=device, device_id_type=MESH
        )

    def b_copy(d):
        return remote(b_buf.at[ka], b_buf.at[ka], b_send.at[d], b_recv.at[d], {"ka": lax.rem(ka + d, GROUP)})

    def c_copy(d):
        return remote(c_buf.at[ja], c_buf.at[ja], c_send.at[d], c_recv.at[d], {"ja": lax.rem(ja + d, GROUP)})

    def b_landed(d):
        slot = lax.rem(ka + GROUP - d, GROUP)
        return remote(b_buf.at[slot], b_buf.at[slot], b_send.at[d], b_recv.at[d], {"ka": slot})

    def c_landed(d):
        slot = lax.rem(ja + GROUP - d, GROUP)
        return remote(c_buf.at[slot], c_buf.at[slot], c_send.at[d], c_recv.at[d], {"ja": slot})

    for d in range(1, GROUP):
        c_copy(d).start()
    for d in range(1, GROUP):
        b_copy(d).start()

    for d in range(1, GROUP):
        b_landed(d).wait_recv()
    bt = b_buf[...].reshape(RANK, DEPTH)
    nt = (((1,), (1,)), ((), ()))
    gram = lax.dot_general(bt, bt, nt, preferred_element_type=jnp.float32)
    for h in range(2):
        gb[pl.ds(h * 32, 32)] = gram[:, h * LANES : (h + 1) * LANES].reshape(32, SUB, LANES)

    def gb_copy(d):
        q = lax.rem(ja + d, GROUP)
        return remote(gb.at[tile_of(q, ka)], gb_in.at[ja], gb_send.at[d], gb_recv.at[d], {"ja": q})

    def gb_landed(d):
        q = lax.rem(ja + GROUP - d, GROUP)
        return remote(gb.at[tile_of(q, ka)], gb_in.at[q], gb_send.at[d], gb_recv.at[d], {"ja": q})

    for d in range(1, GROUP):
        gb_copy(d).start()
    gb_in[ja] = gb[me]

    for d in range(1, GROUP):
        c_landed(d).wait_recv()
    ct = c_buf[...].reshape(RANK, DEPTH)
    first = lax.rem(y, 2) * 4 + ja // 4
    run = jnp.concatenate([c_buf[first], c_buf[first + 2]], axis=0)
    side = c_buf[pl.ds((y // 2) * 4, 4)].reshape(LANES, DEPTH)
    gram = lax.dot_general(run, side, nt, preferred_element_type=jnp.float32)
    gc[...] = gram.reshape(GROUP, SUB, LANES)

    def gc_copy(d):
        q = lax.rem(ka + d, GROUP)
        return remote(gc.at[lax.rem(q, 2) * 4 + q // 2], gc_in.at[ka], gc_send.at[d], gc_recv.at[d], {"ka": q})

    def gc_landed(d):
        q = lax.rem(ka + GROUP - d, GROUP)
        return remote(gc.at[lax.rem(q, 2) * 4 + q // 2], gc_in.at[q], gc_send.at[d], gc_recv.at[d], {"ka": q})

    for d in range(1, GROUP):
        gc_copy(d).start()
    gc_in[ka] = gc[core * 4 + ka // 2]

    b_wide[...] = bt.astype(jnp.float32).T
    c_wide[...] = ct.astype(jnp.float32).T.astype(jnp.bfloat16)

    def contract(n, carry):
        x = t_buf[pl.ds(n * STEP, STEP)].reshape(STEP * DEPTH, DEPTH)
        inner = jnp.dot(x, c_wide[...], preferred_element_type=jnp.float32)
        total = jnp.sum(inner.reshape(STEP, DEPTH, RANK) * b_wide[...][None], axis=1)
        left, right = total[:, :LANES], total[:, LANES:]
        j, k = n // 4, lax.rem(n, 4) * 2
        m_out[tile_of(j, k)] = jnp.concatenate([left[:4], right[:4]], axis=0)
        m_out[tile_of(j, k + 1)] = jnp.concatenate([left[4:], right[4:]], axis=0)
        return carry

    per_chunk = ROWS // STEP // CHUNKS

    def contract_chunk(n):
        load(n).wait()
        lax.fori_loop(0, per_chunk, lambda i, carry: contract(n * per_chunk + i, carry), 0)

    def my_column(dy, e):
        return lax.rem(y + dy, 4) * 2 + (core if e == 0 else 1 - core)

    def my_copy(dy, e):
        p, k = my_column(dy, e), dy * 2 + e
        return remote(
            m_out.at[pl.ds(p * GROUP, GROUP)], my_in.at[column], my_send.at[k], my_recv.at[k], along_y(p)
        )

    def my_landed(dy, e):
        p, k = my_column(4 - dy, e), dy * 2 + e
        return remote(m_out.at[pl.ds(p * GROUP, GROUP)], my_in.at[p], my_send.at[k], my_recv.at[k], along_y(p))

    my_all = [(dy, e) for dy in range(4) for e in range(2) if dy + e > 0]

    contract_chunk(order[0])
    contract_chunk(order[1])
    my_copy(2, 0).start()
    my_copy(2, 1).start()
    contract_chunk(order[2])

    for d in range(1, GROUP):
        gb_landed(d).wait_recv()
        gc_landed(d).wait_recv()
    sum_b = jnp.sum(gb_in[...], axis=0)
    sum_c = jnp.sum(gc_in[...], axis=0)
    my_half = me // 32
    my_row = lax.rem(me, 32) * SUB
    row = lax.broadcasted_iota(jnp.int32, (SUB, LANES), 0) + my_row
    col = lax.broadcasted_iota(jnp.int32, (SUB, LANES), 1) + my_half * LANES
    mine = pl.ds(pl.multiple_of(my_row, SUB), SUB)
    a_ref[my_half, mine, :] = sum_b * sum_c + jnp.where(row == col, RIDGE, 0.0)

    def rows_of(p, q, count):
        start = lax.rem(p, 4) * 64 + q * SUB
        return a_ref.at[p // 4, pl.ds(pl.multiple_of(start, SUB), count * SUB), :]

    def z_at(e, d):
        return lax.rem(z // 4 + e, 2) * 4 + lax.rem(z + d, 4)

    def az_copy(e, d):
        tile, k = rows_of(column, z, 1), e * 4 + d
        return remote(tile, tile, az_send.at[k], az_recv.at[k], along_z(z_at(e, d)))

    def az_landed(e, d):
        q, k = z_at(e, 4 - d), e * 4 + d
        tile = rows_of(column, q, 1)
        return remote(tile, tile, az_send.at[k], az_recv.at[k], along_z(q))

    def ay_copy(e, d):
        tiles = rows_of(column, lax.rem(z // 4 + e, 2) * 4, 4)
        return remote(tiles, tiles, ay_send.at[e, d], ay_recv.at[e, d], along_y(lax.rem(column + d, GROUP)))

    def ay_landed(e, d):
        p = lax.rem(column + GROUP - d, GROUP)
        tiles = rows_of(p, lax.rem(z // 4 + e, 2) * 4, 4)
        return remote(tiles, tiles, ay_send.at[e, d], ay_recv.at[e, d], along_y(p))

    def mz_copy(d):
        p = lax.rem(z + d, GROUP)
        return remote(mz_out.at[p], mz_in.at[z], mz_send.at[d], mz_recv.at[d], along_z(p))

    def mz_landed(d):
        p = lax.rem(z + GROUP - d, GROUP)
        return remote(mz_out.at[p], mz_in.at[p], mz_send.at[d], mz_recv.at[d], along_z(p))

    others = range(1, GROUP)
    az_all = [(e, d) for e in (1, 0) for d in range(4) if e + d > 0]

    def pass_on(e):
        for d in range(4):
            if e + d > 0:
                az_landed(e, d).wait_recv()
        for d in others:
            ay_copy(e, d).start()

    for e, d in az_all:
        az_copy(e, d).start()
    contract_chunk(order[3])
    my_copy(1, 0).start()
    my_copy(1, 1).start()
    contract_chunk(order[4])
    pass_on(0)
    contract_chunk(order[5])
    pass_on(1)
    my_copy(3, 0).start()
    my_copy(3, 1).start()
    contract_chunk(order[6])
    contract_chunk(order[7])
    my_copy(0, 1).start()
    my_in[column] = m_out[pl.ds(column * GROUP, GROUP)]
    for d in others:
        for e in range(2):
            ay_landed(e, d).wait_recv()
    for d in others:
        for e in range(2):
            ay_copy(e, d).wait_send()
    for e, d in az_all:
        az_copy(e, d).wait_send()

    blocks = RANK // PIV
    start_sweep(a_ref, next_ref, w_ref, lhs_ref, rhs_ref)
    sweep(0, 3, a_ref, next_ref, w_ref, lhs_ref, rhs_ref)
    for dy, e in my_all:
        my_landed(dy, e).wait_recv()
    mz_out[...] = jnp.sum(my_in[...], axis=0)
    for d in others:
        mz_copy(d).start()
    mz_in[z] = mz_out[z]
    sweep(3, blocks, a_ref, next_ref, w_ref, lhs_ref, rhs_ref)
    trail(blocks - 1, a_ref, w_ref, lhs_ref, rhs_ref)
    for d in others:
        mz_landed(d).wait_recv()
    total = jnp.sum(mz_in[...], axis=0)
    left, right = total[:4], total[4:]
    for h in range(2):
        part = jnp.dot(left, a_ref[h, pl.ds(0, LANES), :], precision=lax.Precision.HIGHEST,
                       preferred_element_type=jnp.float32)
        part += jnp.dot(right, a_ref[h, pl.ds(LANES, LANES), :], precision=lax.Precision.HIGHEST,
                        preferred_element_type=jnp.float32)
        out_ref[:, h * LANES : (h + 1) * LANES] = -part

    for d in range(1, GROUP):
        b_copy(d).wait_send()
        c_copy(d).wait_send()
        gb_copy(d).wait_send()
        gc_copy(d).wait_send()
        mz_copy(d).wait_send()
    for dy, e in my_all:
        my_copy(dy, e).wait_send()


def body(tensor, factor_b, factor_c):
    f32, bf16 = jnp.float32, jnp.bfloat16
    vmem, dma = pltpu.VMEM, pltpu.SemaphoreType.DMA
    return pl.pallas_call(
        kernel,
        out_shape=jax.ShapeDtypeStruct((4, RANK), f32),
        in_specs=[
            pl.BlockSpec(memory_space=pl.ANY),
            pl.BlockSpec(memory_space=pl.ANY),
            pl.BlockSpec(memory_space=pl.ANY),
        ],
        out_specs=pl.BlockSpec(memory_space=pltpu.VMEM),
        scratch_shapes=[
            vmem((ROWS, DEPTH, DEPTH), bf16),
            vmem((GROUP, RANK // GROUP, DEPTH), bf16),
            vmem((GROUP, RANK // GROUP, DEPTH), bf16),
            vmem((DEPTH, RANK), f32),
            vmem((DEPTH, RANK), bf16),
            vmem((PLANE, SUB, LANES), f32),
            vmem((GROUP, SUB, LANES), f32),
            vmem((GROUP, SUB, LANES), f32),
            vmem((GROUP, SUB, LANES), f32),
            vmem((2, RANK, LANES), f32),
            vmem((PLANE, SUB, LANES), f32),
            vmem((GROUP, GROUP, SUB, LANES), f32),
            vmem((GROUP, SUB, LANES), f32),
            vmem((GROUP, SUB, LANES), f32),
            vmem((2, PIV, LANES), f32),
            vmem((2, PIV, LANES), f32),
            vmem((RANK, 6 * PIV), bf16),
            vmem((6 * PIV, RANK), bf16),
            dma((2,)),
            dma((CHUNKS,)),
            *[dma((GROUP,)) for _ in range(10)],
            *[dma((2, GROUP)) for _ in range(2)],
            *[dma((GROUP,)) for _ in range(4)],
        ],
        compiler_params=pltpu.CompilerParams(collective_id=0, has_side_effects=True),
        name="factor_update",
    )(tensor, factor_b.T, factor_c.T)


def solution(mesh):
    return jax.shard_map(
        body,
        mesh=mesh,
        in_specs=(P("ia", "ja", "ka"), P("ja", "ka"), P("ka", "ja")),
        out_specs=P(("ia", "ja", "ka"), None),
        check_vma=False,
    )
```
